256 devices in a mesh: pipe: 8 (over x, core), expert: 32 (over y, z).
Axes of the slice: x: 4, y: 4, z: 8, core: 2. Of those that a mesh axis runs over, the one named last changes fastest.
Arguments:
- x_in: bfloat16 [4, 192, 3584], P(None, 'expert'), may hold values from -6 to 6
- grad_in: bfloat16 [4, 192, 3584], P(None, 'expert'), may hold values from -6 to 6
- norm_gain: float32 [8, 3584], P('pipe'), may hold values from 0.1 to 1.9
- w_in: bfloat16 [8, 3584, 16384], P('pipe', None, 'expert'), may hold values from -0.09375 to 0.09375
- w_down: bfloat16 [8, 8192, 3584], P('pipe', 'expert'), may hold values from -0.1875 to 0.1875
- routes: int32 [8, 4, 192, 2], P('pipe', None, 'expert'), may hold values from 0 to 7, all different within a row; in each aligned block of 6 rows (0 to 5, 6 to 11, ..., all dimensions but the last counted through in order) at most 2 rows name the same one
- gates: float32 [8, 4, 192, 2], P('pipe', None, 'expert'), may hold values from 0.2 to 1.2
Outputs:
- acts: bfloat16 [8, 4, 192, 3584], P('pipe', None, 'expert')
- grads: bfloat16 [8, 4, 192, 3584], P('pipe', None, 'expert')
The draws below stay inside these ranges and needn't reach their ends.
Inputs may be any that keep to these rules, and one draw needn't show every extreme that they name: `routes`: in each aligned block of 6 rows (one device's tokens of one section and micro-batch) no expert is named by more than 2 rows; the 2 experts of a row differ.
All inputs are finite; a program needn't handle non-finite values.
Results may differ from the reference program's by a relative error of at most 0.04.
Values may be sent and summed in bfloat16 or wider, within the bound.
A program may use at most 64 MiB of HBM per device.

```python
import math
import jax
import jax.numpy as jnp
import numpy as np
from jax import lax

D = 3584
FF = 1024
GROUP = 4
TOPK = 2
MICRO = 4
TOK_DEV = 6
H_DEV = 256
EXPERTS = 8
TOKENS = 192
CAP = 2
N_PIPE = 8
N_EXPERT = 32


def steps_of(own_key, extent, split, least, largest):
    level, own = 1.0, jax.random.fold_in(own_key, 6)
    for position, blocks in split:
        steps = jnp.exp(jax.random.uniform(jax.random.fold_in(own, position), (blocks,), jnp.float32, least / len(split), largest / len(split)))
        level = level * jnp.repeat(steps, extent[position] // blocks).reshape([-1 if axis == position else 1 for axis in range(len(extent))])
    return level


def routed_block(own_key, own, number, rows, amount, top, most, lean):
    ranking = jax.random.permutation(own_key, amount)
    packed, usual = portions_of(amount, rows * top, most, lean, True), portions_of(amount, rows * top, most, lean, False)
    places = jnp.arange(amount)

    def named(lengths, turn):
        used = int((lengths > 0).sum())
        fixed = max(1, used // 4)
        moved = fixed + (places - fixed + turn * (used - fixed)) % max(1, amount - fixed)
        return jnp.zeros((amount,), jnp.int32).at[ranking[jnp.where(places < fixed, places, moved)]].set(jnp.asarray(lengths, jnp.int32))

    lengths = jnp.where(number % 4 == 0, named(packed, number // 4), named(usual, number - number // 4 - 1))
    mixed = jax.random.permutation(jax.random.fold_in(own, 3), amount)
    giver, sink = mixed[0:amount // 2 * 2:2], mixed[1:amount // 2 * 2:2]
    slack = jnp.minimum(lengths[giver] - 1, most - lengths[sink]) // 2
    slack = jnp.where((giver == ranking[0]) | (sink == ranking[0]) | (lengths[sink] == 0), 0, jnp.maximum(slack, 0))
    moved = jax.random.randint(jax.random.fold_in(own, 4), (amount // 2,), 0, 1 << 20) % (slack + 1)
    lengths = lengths.at[giver].add(-moved).at[sink].add(moved)
    items = jnp.searchsorted(jnp.cumsum(lengths), jnp.arange(rows * top), side="right").astype(jnp.int32)
    listing = items.reshape(top, rows).T
    listing = listing[jax.random.permutation(jax.random.fold_in(own, 1), rows)]
    turn = jax.random.randint(jax.random.fold_in(own, 2), (rows, 1), 0, top)
    return jnp.take_along_axis(listing, (jnp.arange(top)[None, :] + turn) % top, axis=1)


def portions_of(amount, total, bound, slope, full):
    loads = [(1 << 20) // math.isqrt(standing ** slope) + 1 for standing in range(1, amount + 1)]
    largest = bound if full else min(bound, max(-(-total // amount), total * loads[0] // sum(loads)))
    least = 1 if total - largest >= amount - 1 else 0
    counts, spare = [largest] + [least] * (amount - 1), total - largest - least * (amount - 1)
    while spare > 0:
        candidates = [i for i in range(1, amount) if counts[i] < largest] or [i for i in range(1, amount) if counts[i] < bound]
        whole, budget = sum([loads[i] for i in candidates]), spare
        for i in candidates:
            addition = min(bound - counts[i], max(1, budget * loads[i] // whole), spare)
            counts[i] = counts[i] + addition
            spare = spare - addition
    return np.array(counts)


def scatter_about(rng, extent, width, bound, pieces=(), kind=jnp.bfloat16):
    values = width * jax.random.normal(rng, extent, jnp.float32)
    if pieces:
        values = values * steps_of(rng, extent, pieces, -0.22, 0.18)
    return jnp.clip(values, -bound, bound).astype(kind)


def setup_inputs(seed: int = 0) -> dict:
    arg_keys = jax.random.split(jax.random.key(seed), 8)
    x_in = scatter_about(arg_keys[0], (MICRO, TOKENS, D), 1.0, 6.0, ((1, 32),))
    grad_in = scatter_about(arg_keys[1], (MICRO, TOKENS, D), 1.0, 6.0, ((1, 32),))
    norm_gain = jnp.clip(1.0 + 0.18 * jax.random.normal(arg_keys[2], (N_PIPE, D), jnp.float32), 0.1, 1.9)
    w_in = scatter_about(arg_keys[3], (N_PIPE, D, 2 * N_EXPERT * H_DEV), D ** -0.5, 0.09375, ((0, 8), (2, 32)))
    w_down = scatter_about(arg_keys[4], (N_PIPE, N_EXPERT * H_DEV, D), FF ** -0.5, 0.1875, ((0, 8), (1, 32)))
    routes_keys = jax.random.split(jax.random.fold_in(arg_keys[5], 1), N_PIPE * MICRO * TOKENS // TOK_DEV)
    routes_turns = jax.random.permutation(jax.random.fold_in(arg_keys[5], 3), N_PIPE * MICRO * TOKENS // TOK_DEV)
    routes = jax.vmap(lambda own, number: routed_block(jax.random.fold_in(arg_keys[5], 2), own, number, TOK_DEV, EXPERTS, TOPK, CAP, 2))(routes_keys, routes_turns).reshape((N_PIPE, MICRO, TOKENS, TOPK))
    gates = jnp.clip(0.2 + 1 * jax.random.uniform(arg_keys[6], (N_PIPE, MICRO, TOKENS, TOPK), jnp.float32) ** steps_of(arg_keys[6], (N_PIPE, MICRO, TOKENS, TOPK), ((0, 8), (2, 32)), -0.2, 0.2), 0.2, 1.2)
    return {"x_in": x_in, "grad_in": grad_in, "norm_gain": norm_gain, "w_in": w_in, "w_down": w_down, "routes": routes, "gates": gates}


norm_eps = 1e-06
exact_mode = lax.Precision.HIGHEST

def rounded(values):
    return lax.optimization_barrier(values.astype(jnp.bfloat16)).astype(jnp.float32)

def section_weights(w_in, w_down, section_idx):
    joined = w_in[section_idx].astype(jnp.float32).reshape(D, EXPERTS, GROUP, 2, H_DEV)
    down_rows = w_down[section_idx].astype(jnp.float32).reshape(EXPERTS, GROUP, H_DEV, D)
    return (joined[:, :, :, 0, :], joined[:, :, :, 1, :], down_rows)

def mixing_table(routes, gates, section_idx, micro_idx):
    labels = jnp.arange(EXPERTS, dtype=jnp.int32)
    chosen = (routes[section_idx, micro_idx][:, :, None] == labels[None, None, :]).astype(jnp.float32)
    return lax.optimization_barrier(jnp.sum(gates[section_idx, micro_idx][:, :, None] * chosen, axis=1))

def project(hidden_in, gain_row, gate_cols, up_cols):
    values = hidden_in.astype(jnp.float32)
    inv_rms = lax.rsqrt(lax.optimization_barrier(jnp.mean(values * values, axis=-1, keepdims=True)) + norm_eps)
    normed = rounded(values * inv_rms * gain_row)
    pre_gate = jnp.einsum('td,degh->tegh', normed, gate_cols, precision=exact_mode)
    pre_up = jnp.einsum('td,degh->tegh', normed, up_cols, precision=exact_mode)
    return (values, inv_rms, pre_gate, pre_up)

def layer_forward(hidden_in, gain_row, gate_cols, up_cols, down_rows, mixing):
    values, inv_rms, pre_gate, pre_up = project(hidden_in, gain_row, gate_cols, up_cols)
    inner = rounded(jax.nn.silu(pre_gate) * pre_up)
    part_out = rounded(jnp.einsum('tegh,eghd->tegd', inner, down_rows, precision=exact_mode))
    totals = lax.optimization_barrier(jnp.sum(part_out, axis=2))
    branch = jnp.einsum('te,ted->td', mixing, totals, precision=exact_mode)
    return (values + branch).astype(jnp.bfloat16)

def layer_backward(hidden_in, grad_out, gain_row, gate_cols, up_cols, down_rows, mixing):
    values, inv_rms, pre_gate, pre_up = project(hidden_in, gain_row, gate_cols, up_cols)
    grad_vals = grad_out.astype(jnp.float32)
    scaled = rounded(mixing[:, :, None] * grad_vals[:, None, :])
    d_inner = jnp.einsum('ted,eghd->tegh', scaled, down_rows, precision=exact_mode)
    sigma = jax.nn.sigmoid(pre_gate)
    d_gate = rounded(d_inner * pre_up * sigma * (1.0 + pre_gate * (1.0 - sigma)))
    d_up = rounded(d_inner * pre_gate * sigma)
    d_part = jnp.einsum('tegh,degh->tegd', d_gate, gate_cols, precision=exact_mode)
    d_part = rounded(d_part + jnp.einsum('tegh,degh->tegd', d_up, up_cols, precision=exact_mode))
    d_normed = lax.optimization_barrier(jnp.sum(d_part, axis=(1, 2)))
    d_scaled = d_normed * gain_row
    inner_prod = lax.optimization_barrier(jnp.sum(d_scaled * values, axis=-1, keepdims=True))
    result = grad_vals + inv_rms * d_scaled - inv_rms * inv_rms * inv_rms * values * inner_prod / D
    return result.astype(jnp.bfloat16)

def reference(x_in, grad_in, norm_gain, w_in, w_down, routes, gates):
    inputs_all = [[None] * MICRO for section_idx in range(N_PIPE)]
    acts_all = [[None] * MICRO for section_idx in range(N_PIPE)]
    grads_all = [[None] * MICRO for section_idx in range(N_PIPE)]
    for section_idx in range(N_PIPE):
        gate_cols, up_cols, down_rows = section_weights(w_in, w_down, section_idx)
        for micro_idx in range(MICRO):
            hidden_in = x_in[micro_idx] if section_idx == 0 else acts_all[section_idx - 1][micro_idx]
            inputs_all[section_idx][micro_idx] = hidden_in
            mixing = mixing_table(routes, gates, section_idx, micro_idx)
            acts_all[section_idx][micro_idx] = layer_forward(hidden_in, norm_gain[section_idx], gate_cols, up_cols, down_rows, mixing)
    for section_idx in range(N_PIPE - 1, -1, -1):
        gate_cols, up_cols, down_rows = section_weights(w_in, w_down, section_idx)
        for micro_idx in range(MICRO):
            grad_out = grad_in[micro_idx] if section_idx == N_PIPE - 1 else grads_all[section_idx + 1][micro_idx]
            mixing = mixing_table(routes, gates, section_idx, micro_idx)
            grads_all[section_idx][micro_idx] = layer_backward(inputs_all[section_idx][micro_idx], grad_out, norm_gain[section_idx], gate_cols, up_cols, down_rows, mixing)
    acts = jnp.stack([jnp.stack(row) for row in acts_all])
    grads = jnp.stack([jnp.stack(row) for row in grads_all])
    return (acts, grads)
```

```python
import jax
import jax.numpy as jnp
from jax import lax
from jax.sharding import PartitionSpec as P

GROUP = 4


norm_eps = 1e-06
exact_mode = lax.Precision.HIGHEST


def from_behind(block, axis, distance):
    devices = range(lax.axis_size(axis))
    route = [(i - distance, i) for i in devices if i - distance in devices]
    return lax.ppermute(block, axis, route)


def local(x_in, grad_in, norm_gain, w_in, w_down, routes, gates):
    sections = lax.axis_size("pipe")
    section_idx = lax.axis_index("pipe")
    devices = lax.axis_size("expert")
    experts = devices // GROUP
    micro_count = x_in.shape[0]
    tok_count = x_in.shape[1]
    width = x_in.shape[2]
    topk_count = routes.shape[-1]
    unit_count = w_down.shape[1]
    capacity = min(tok_count, max(2, tok_count * topk_count // experts + 1))
    slot_count = devices * capacity
    gain_row = norm_gain[0]
    weights_in = w_in[0]
    weights_down = w_down[0]
    contract_last = (((1,), (1,)), ((), ()))

    def tables(micro_idx):
        route_ids = lax.dynamic_index_in_dim(routes[0], micro_idx, 0, keepdims=False).reshape(-1)
        weight_ids = lax.dynamic_index_in_dim(gates[0], micro_idx, 0, keepdims=False).reshape(-1)
        labels = jnp.arange(experts, dtype=jnp.int32)
        onehot = (route_ids[:, None] == labels[None, :]).astype(jnp.int32)
        pairs = jnp.arange(tok_count * topk_count, dtype=jnp.int32)
        ahead = (pairs[None, :] < pairs[:, None]) & (route_ids[None, :] == route_ids[:, None])
        position = jnp.sum(ahead.astype(jnp.int32), axis=1)
        slot_ids = route_ids * capacity + position
        select = (
            slot_ids[:, None] == jnp.arange(experts * capacity, dtype=jnp.int32)[None, :]
        ).astype(jnp.float32)
        pair_tokens = jnp.arange(tok_count * topk_count, dtype=jnp.int32) // topk_count
        owner = (pair_tokens[:, None] == jnp.arange(tok_count, dtype=jnp.int32)[None, :]).astype(
            jnp.float32
        )
        spread = jnp.dot(select.T, owner, precision=exact_mode)
        mixing = jnp.dot(owner.T, select * weight_ids[:, None], precision=exact_mode)
        return (spread, mixing)

    def send(buffer):
        copies = jnp.broadcast_to(
            buffer.reshape(experts, 1, capacity, width), (experts, GROUP, capacity, width)
        )
        return lax.all_to_all(
            copies.reshape(slot_count, width), "expert", split_axis=0, concat_axis=0, tiled=True
        )

    def collect(part_rows):
        returned = lax.all_to_all(part_rows, "expert", split_axis=0, concat_axis=0, tiled=True)
        return jnp.sum(
            returned.astype(jnp.float32).reshape(experts, GROUP, capacity, width), axis=1
        ).reshape(experts * capacity, width)

    def normalize(hidden_in):
        values = hidden_in.astype(jnp.float32)
        inv_rms = lax.rsqrt(jnp.mean(values * values, axis=-1, keepdims=True) + norm_eps)
        return (values, inv_rms)

    def forward_layer(hidden_in, micro_idx):
        spread, mixing = tables(micro_idx)
        values, inv_rms = normalize(hidden_in)
        normed = (values * inv_rms * gain_row).astype(jnp.bfloat16)
        buffer = jnp.dot(
            spread.astype(jnp.bfloat16), normed, preferred_element_type=jnp.float32
        ).astype(jnp.bfloat16)
        rows = send(buffer)
        projected = jnp.dot(rows, weights_in, preferred_element_type=jnp.float32)
        inner = (jax.nn.silu(projected[:, :unit_count]) * projected[:, unit_count:]).astype(
            jnp.bfloat16
        )
        part_rows = jnp.dot(inner, weights_down, preferred_element_type=jnp.float32).astype(
            jnp.bfloat16
        )
        totals = collect(part_rows)
        branch = jnp.dot(mixing, totals, precision=exact_mode)
        return ((values + branch).astype(jnp.bfloat16), rows)

    def backward_layer(hidden_in, grad_out, stored, micro_idx):
        spread, mixing = tables(micro_idx)
        values, inv_rms = normalize(hidden_in)
        grad_vals = grad_out.astype(jnp.float32)
        scaled = jnp.dot(mixing.T, grad_vals, precision=exact_mode).astype(jnp.bfloat16)
        grad_rows = send(scaled)
        projected = jnp.dot(stored, weights_in, preferred_element_type=jnp.float32)
        pre_gate = projected[:, :unit_count]
        pre_up = projected[:, unit_count:]
        d_inner = lax.dot_general(
            grad_rows, weights_down, contract_last, preferred_element_type=jnp.float32
        )
        sigma = jax.nn.sigmoid(pre_gate)
        d_gate = d_inner * pre_up * sigma * (1.0 + pre_gate * (1.0 - sigma))
        d_up = d_inner * pre_gate * sigma
        d_both = jnp.concatenate([d_gate, d_up], axis=1).astype(jnp.bfloat16)
        d_part = lax.dot_general(
            d_both, weights_in, contract_last, preferred_element_type=jnp.float32
        ).astype(jnp.bfloat16)
        totals = collect(d_part)
        d_normed = jnp.dot(spread.T, totals, precision=exact_mode)
        d_scaled = d_normed * gain_row
        inner_prod = jnp.sum(d_scaled * values, axis=-1, keepdims=True)
        result = (
            grad_vals
            + inv_rms * d_scaled
            - inv_rms * inv_rms * inv_rms * values * inner_prod / width
        )
        return result.astype(jnp.bfloat16)

    def place(buffer, item, micro_idx, valid):
        previous = lax.dynamic_index_in_dim(buffer, micro_idx, 0, keepdims=False)
        return lax.dynamic_update_index_in_dim(
            buffer, jnp.where(valid, item, previous), micro_idx, 0
        )

    def forward_tick(tick, carry):
        inbox, acts, inputs, stored_all = carry
        micro_raw = tick - section_idx
        valid = (micro_raw >= 0) & (micro_raw < micro_count)
        micro_idx = jnp.clip(micro_raw, 0, micro_count - 1)
        fresh = lax.dynamic_index_in_dim(x_in, micro_idx, 0, keepdims=False)
        hidden_in = jnp.where(section_idx == 0, fresh, inbox)
        output, stored = forward_layer(hidden_in, micro_idx)
        acts = place(acts, output, micro_idx, valid)
        inputs = place(inputs, hidden_in, micro_idx, valid)
        stored_all = place(stored_all, stored, micro_idx, valid)
        inbox = from_behind(output, "pipe", 1)
        return (inbox, acts, inputs, stored_all)

    def backward_tick(tick, carry):
        inbox, grads = carry
        micro_raw = tick - (sections - 1 - section_idx)
        valid = (micro_raw >= 0) & (micro_raw < micro_count)
        micro_idx = jnp.clip(micro_raw, 0, micro_count - 1)
        fresh = lax.dynamic_index_in_dim(grad_in, micro_idx, 0, keepdims=False)
        grad_out = jnp.where(section_idx == sections - 1, fresh, inbox)
        hidden_in = lax.dynamic_index_in_dim(inputs, micro_idx, 0, keepdims=False)
        stored = lax.dynamic_index_in_dim(stored_all, micro_idx, 0, keepdims=False)
        result = backward_layer(hidden_in, grad_out, stored, micro_idx)
        grads = place(grads, result, micro_idx, valid)
        inbox = from_behind(result, "pipe", -1)
        return (inbox, grads)

    tick_count = micro_count + sections - 1
    empty_rows = jnp.zeros((tok_count, width), jnp.bfloat16)
    empty_acts = jnp.zeros((micro_count, tok_count, width), jnp.bfloat16)
    empty_store = jnp.zeros((micro_count, slot_count, width), jnp.bfloat16)
    final_box, acts, inputs, stored_all = lax.fori_loop(
        0, tick_count, forward_tick, (empty_rows, empty_acts, empty_acts, empty_store)
    )
    final_grad, grads = lax.fori_loop(0, tick_count, backward_tick, (empty_rows, empty_acts))
    return (acts[None], grads[None])


def solution(mesh):
    placed = (
        P(None, "expert", None),
        P(None, "expert", None),
        P("pipe", None),
        P("pipe", None, "expert"),
        P("pipe", "expert", None),
        P("pipe", None, "expert", None),
        P("pipe", None, "expert", None),
    )
    return jax.shard_map(
        local,
        mesh=mesh,
        in_specs=placed,
        out_specs=(P("pipe", None, "expert", None), P("pipe", None, "expert", None)),
        check_vma=False,
    )
```

```python
import jax
import jax.numpy as jnp
from jax import lax
from jax.experimental import pallas as pl
from jax.experimental.pallas import tpu as pltpu
from jax.sharding import PartitionSpec as P

MESH = pl.DeviceIdType.MESH
GROUP = 4
CAP = 2
LANES = 128
ROWS = 8
WIDE = 512
norm_eps = 1e-06
BF = jnp.bfloat16
F32 = jnp.float32


def layer_kernel(
    x_hbm, gin_hbm, gain_ref, win_hbm, wdn_hbm, routes, gates,
    acts_ref, grads_ref,
    win, wdn, win_t, wdn_t, xbuf, hid, gout, aout, bout,
    send_f, rows_f, out_f, ret_f, send_b, rows_b, out_b, ret_b, fac_a, fac_b,
    wsem, xsem, recv, sent, hop_recv, hop_sent,
):
    sections = lax.axis_size("pipe")
    peers = lax.axis_size("expert")
    s = lax.axis_index("pipe")
    d = lax.axis_index("expert")
    micros, tokens, width = xbuf.shape
    topk = routes.shape[-1]
    units = wdn.shape[0]
    tiles = width // LANES
    slots = send_f.shape[2] * CAP
    pairs = peers * CAP
    last = sections - 1

    load_in = pltpu.make_async_copy(win_hbm.at[0], win, wsem.at[0])
    load_down = pltpu.make_async_copy(wdn_hbm.at[0], wdn, wsem.at[1])
    load_x = pltpu.make_async_copy(x_hbm, xbuf, xsem)
    load_g = pltpu.make_async_copy(gin_hbm, xbuf, xsem)

    @pl.when(s == 0)
    def _():
        load_x.start()

    @pl.when(s == last)
    def _():
        load_g.start()

    load_in.start()
    load_down.start()

    barrier = pltpu.get_barrier_semaphore()

    def greet(i, carry):
        pl.semaphore_signal(barrier, inc=1, device_id=(s, lax.rem(d + i, peers)), device_id_type=MESH)
        return carry

    lax.fori_loop(1, peers, greet, 0)

    @pl.when(s > 0)
    def _():
        pl.semaphore_signal(barrier, inc=1, device_id=(s - 1, d), device_id_type=MESH)

    @pl.when(s < last)
    def _():
        pl.semaphore_signal(barrier, inc=1, device_id=(s + 1, d), device_id_type=MESH)

    pl.semaphore_wait(barrier, peers - 1 + jnp.minimum(s, 1) + jnp.minimum(last - s, 1))

    def spread_rows(dest, m):
        dest[m] = jnp.zeros((ROWS, width), BF)
        dest[m, 0:tokens, :] = xbuf[m]

    @pl.when(s == 0)
    def _():
        load_x.wait()
        for m in range(micros):
            spread_rows(hid, m)

    @pl.when(s == last)
    def _():
        load_g.wait()
        for m in range(micros):
            spread_rows(gout, m)

    def chosen(m):
        ids = [routes[0, m, p // topk, p % topk] for p in range(tokens * topk)]
        found = []
        for p, e in enumerate(ids):
            place = jnp.int32(0)
            for q in range(p):
                place = place + jnp.where(ids[q] == e, 1, 0)
            found.append((p // topk, e * CAP + place, gates[0, m, p // topk, p % topk]))
        return found

    def by_slot(m, weighted):
        count = 2 * slots if weighted else slots
        row = lax.broadcasted_iota(jnp.int32, (count, ROWS), 0)
        col = lax.broadcasted_iota(jnp.int32, (count, ROWS), 1)
        table = jnp.zeros((count, ROWS), F32)
        for t, slot, gate in chosen(m):
            hit = (lax.rem(row, slots) == slot) & (col == t)
            table = jnp.where(hit, gate if weighted else 1.0, table)
        if weighted:
            high = table.astype(BF).astype(F32)
            table = jnp.where(row < slots, high, table - high)
        return table.astype(BF)

    def by_token(m, weighted):
        count = 2 * ROWS if weighted else ROWS
        row = lax.broadcasted_iota(jnp.int32, (count, pairs), 0)
        col = lax.broadcasted_iota(jnp.int32, (count, pairs), 1)
        slot_of = (col // (GROUP * CAP)) * CAP + lax.rem(col, CAP)
        table = jnp.zeros((count, pairs), F32)
        for t, slot, gate in chosen(m):
            hit = (slot_of == slot) & (lax.rem(row, ROWS) == t)
            table = jnp.where(hit, gate if weighted else 1.0, table)
        if weighted:
            high = table.astype(BF).astype(F32)
            table = jnp.where(row < ROWS, high, table - high)
        return table.astype(BF)

    def dispatch(send, rows, m, phase):
        def start(i, carry):
            peer = lax.rem(d + i, peers)
            pltpu.make_async_remote_copy(
                src_ref=send.at[m, :, peer // GROUP],
                dst_ref=rows.at[m, :, d],
                send_sem=sent.at[phase, m],
                recv_sem=recv.at[phase, m],
                device_id=(s, peer),
                device_id_type=MESH,
            ).start()
            return carry

        lax.fori_loop(1, peers, start, 0)
        pltpu.make_async_copy(send.at[m, :, d // GROUP], rows.at[m, :, d], recv.at[phase, m]).start()

    def give_back(out, ret, m, phase):
        def start(i, carry):
            peer = lax.rem(d + i, peers)
            pltpu.make_async_remote_copy(
                src_ref=out.at[m, :, peer],
                dst_ref=ret.at[m, :, d],
                send_sem=sent.at[phase, m],
                recv_sem=recv.at[phase, m],
                device_id=(s, peer),
                device_id_type=MESH,
            ).start()
            return carry

        lax.fori_loop(1, peers, start, 0)
        pltpu.make_async_copy(out.at[m, :, d], ret.at[m, :, d], recv.at[phase, m]).start()

    def arrived(buf, m, phase):
        pltpu.make_async_copy(buf.at[m], buf.at[m], recv.at[phase, m]).wait()

    def flat(buf, m, count):
        view = buf.at[m].reshape(tiles, count, LANES)
        return jnp.concatenate([view[k] for k in range(tiles)], axis=1)

    def store_flat(buf, m, count, first, value):
        view = buf.at[m].reshape(tiles, count, LANES)
        for k in range(value.shape[1] // LANES):
            view[first + k] = value[:, k * LANES : (k + 1) * LANES]

    def hop(src, dst, m, way, to):
        return pltpu.make_async_remote_copy(
            src_ref=src.at[m],
            dst_ref=dst.at[m],
            send_sem=hop_sent.at[way, m],
            recv_sem=hop_recv.at[way, m],
            device_id=(to, d),
            device_id_type=MESH,
        )

    def normalize(m):
        values = hid[m].astype(F32)
        inv = lax.rsqrt(jnp.mean(values * values, axis=1, keepdims=True) + norm_eps)
        return values, inv

    def turn_weights():
        for k in range(0, width, WIDE):
            win_t[:, k : k + WIDE] = win[k : k + WIDE, :].T
            wdn_t[k : k + WIDE, :] = wdn[:, k : k + WIDE].T

    load_in.wait()
    load_down.wait()

    @pl.when(s > 0)
    def _():
        turn_weights()

    def forward(m, carry):
        @pl.when(s > 0)
        def _():
            hop(aout, hid, m, 0, s).wait_recv()

        values, inv = normalize(m)
        normed = (values * inv * gain_ref[...]).astype(BF)
        block = jnp.dot(by_slot(m, False), normed, preferred_element_type=F32)
        store_flat(send_f, m, slots, 0, block.astype(BF))
        dispatch(send_f, rows_f, m, 0)
        arrived(rows_f, m, 0)
        pre = jnp.dot(flat(rows_f, m, pairs), win[...], preferred_element_type=F32)
        gate, up = pre[:, :units], pre[:, units:]
        sigma = jax.nn.sigmoid(gate)
        inner = (gate * sigma * up).astype(BF)
        for k in range(0, width, WIDE):
            part = jnp.dot(inner, wdn[:, k : k + WIDE], preferred_element_type=F32)
            store_flat(out_f, m, pairs, k // LANES, part.astype(BF))
        give_back(out_f, ret_f, m, 1)
        fac_a[m] = up * sigma * (1.0 + gate * (1.0 - sigma))
        fac_b[m] = gate * sigma
        table = by_token(m, True)
        arrived(ret_f, m, 1)
        both = jnp.dot(table, flat(ret_f, m, pairs), preferred_element_type=F32)
        result = (hid[m].astype(F32) + (both[:ROWS] + both[ROWS:])).astype(BF)
        aout[m] = result

        @pl.when(s < last)
        def _():
            hop(aout, hid, m, 0, s + 1).start()

        acts_ref[0, m] = result[:tokens]
        return carry

    lax.fori_loop(0, micros, forward, 0)

    @pl.when(s == 0)
    def _():
        turn_weights()

    def backward(m, carry):
        @pl.when(s < last)
        def _():
            hop(bout, gout, m, 1, s).wait_recv()

        block = jnp.dot(by_slot(m, True), gout[m], preferred_element_type=F32)
        store_flat(send_b, m, slots, 0, (block[:slots] + block[slots:]).astype(BF))
        dispatch(send_b, rows_b, m, 2)
        arrived(rows_b, m, 2)
        d_inner = jnp.dot(flat(rows_b, m, pairs), wdn_t[...], preferred_element_type=F32)
        d_both = jnp.concatenate([d_inner * fac_a[m], d_inner * fac_b[m]], axis=1).astype(BF)
        for k in range(0, width, WIDE):
            part = jnp.dot(d_both, win_t[:, k : k + WIDE], preferred_element_type=F32)
            store_flat(out_b, m, pairs, k // LANES, part.astype(BF))
        give_back(out_b, ret_b, m, 3)
        values, inv = normalize(m)
        table = by_token(m, False)
        arrived(ret_b, m, 3)
        d_normed = jnp.dot(table, flat(ret_b, m, pairs), preferred_element_type=F32)
        d_scaled = d_normed * gain_ref[...]
        product = jnp.sum(d_scaled * values, axis=1, keepdims=True)
        result = gout[m].astype(F32) + inv * d_scaled - (inv * inv * inv * product / width) * values
        result = result.astype(BF)
        bout[m] = result

        @pl.when(s > 0)
        def _():
            hop(bout, gout, m, 1, s - 1).start()

        grads_ref[0, m] = result[:tokens]
        return carry

    lax.fori_loop(0, micros, backward, 0)

    def settle(m, carry):
        for phase in range(4):
            most = out_f.at[m, :, 0 : peers - 1]
            pltpu.make_async_copy(most, most, sent.at[phase, m]).wait()

        @pl.when(s < last)
        def _():
            hop(aout, hid, m, 0, s + 1).wait_send()

        @pl.when(s > 0)
        def _():
            hop(bout, gout, m, 1, s - 1).wait_send()

        return carry

    lax.fori_loop(0, micros, settle, 0)


def local(x_in, grad_in, norm_gain, w_in, w_down, routes, gates):
    peers = lax.axis_size("expert")
    micros, tokens, width = x_in.shape
    cols = w_in.shape[2]
    units = w_down.shape[1]
    tiles = width // LANES
    out = jax.ShapeDtypeStruct((1, micros, tokens, width), BF)
    small = pltpu.VMEM((micros, tiles, peers // GROUP, CAP, LANES), BF)
    large = pltpu.VMEM((micros, tiles, peers, CAP, LANES), BF)
    state = pltpu.VMEM((micros, ROWS, width), BF)
    factor = pltpu.VMEM((micros, peers * CAP, units), F32)
    anywhere = pl.BlockSpec(memory_space=pl.ANY)
    vmem = pl.BlockSpec(memory_space=pltpu.VMEM)
    smem = pl.BlockSpec(memory_space=pltpu.SMEM)
    return pl.pallas_call(
        layer_kernel,
        out_shape=(out, out),
        in_specs=[anywhere, anywhere, vmem, anywhere, anywhere, smem, smem],
        out_specs=(vmem, vmem),
        scratch_shapes=[
            pltpu.VMEM((width, cols), BF),
            pltpu.VMEM((units, width), BF),
            pltpu.VMEM((cols, width), BF),
            pltpu.VMEM((width, units), BF),
            pltpu.VMEM((micros, tokens, width), BF),
            state, state, state, state,
            small, large, large, large,
            small, large, large, large,
            factor, factor,
            pltpu.SemaphoreType.DMA((2,)),
            pltpu.SemaphoreType.DMA,
            pltpu.SemaphoreType.DMA((4, micros)),
            pltpu.SemaphoreType.DMA((4, micros)),
            pltpu.SemaphoreType.DMA((2, micros)),
            pltpu.SemaphoreType.DMA((2, micros)),
        ],
        compiler_params=pltpu.CompilerParams(
            collective_id=0, has_side_effects=True, vmem_limit_bytes=56 << 20
        ),
    )(x_in, grad_in, norm_gain, w_in, w_down, routes, gates)


def solution(mesh):
    placed = (
        P(None, "expert", None),
        P(None, "expert", None),
        P("pipe", None),
        P("pipe", None, "expert"),
        P("pipe", "expert", None),
        P("pipe", None, "expert", None),
        P("pipe", None, "expert", None),
    )
    return jax.shard_map(
        local,
        mesh=mesh,
        in_specs=placed,
        out_specs=(P("pipe", None, "expert", None), P("pipe", None, "expert", None)),
        check_vma=False,
    )
```

```python
import jax
import jax.numpy as jnp
from jax import lax
from jax.experimental import pallas as pl
from jax.experimental.pallas import tpu as pltpu
from jax.sharding import PartitionSpec as P

MESH = pl.DeviceIdType.MESH
GROUP = 4
CAP = 2
LANES = 128
ROWS = 8
WIDE = 512
NY = 4
NZ = 8
CHUNKS = 2
norm_eps = 1e-06
BF = jnp.bfloat16
F32 = jnp.float32


def layer_kernel(
    x_hbm, gin_hbm, gain_ref, win_hbm, wdn_hbm, routes, gates,
    acts_ref, grads_ref,
    win, wdn, win_t, wdn_t, xbuf, hid, gout, aout, bout,
    send_f, rows_f, out_f, ret_f, send_b, rows_b, out_b, ret_b, fac_a, fac_b,
    wsem, xsem, recv, sent, hop_recv, hop_sent,
):
    sections = lax.axis_size("pipe")
    peers = lax.axis_size("expert")
    s = lax.axis_index("pipe")
    d = lax.axis_index("expert")
    micros, tokens, width = xbuf.shape
    topk = routes.shape[-1]
    units = wdn.shape[0]
    tiles = width // LANES
    slots = send_f.shape[2] * CAP
    pairs = peers * CAP
    last = sections - 1
    span = peers // CHUNKS
    y, z = d >> 3, d & (NZ - 1)

    load_in = pltpu.make_async_copy(win_hbm.at[0], win, wsem.at[0])
    load_down = pltpu.make_async_copy(wdn_hbm.at[0], wdn, wsem.at[1])
    load_x = pltpu.make_async_copy(x_hbm, xbuf, xsem)
    load_g = pltpu.make_async_copy(gin_hbm, xbuf, xsem)

    @pl.when(s == 0)
    def _():
        load_x.start()

    @pl.when(s == last)
    def _():
        load_g.start()

    load_in.start()
    load_down.start()

    barrier = pltpu.get_barrier_semaphore()

    def greet(i, carry):
        pl.semaphore_signal(barrier, inc=1, device_id=(s, lax.rem(d + i, peers)), device_id_type=MESH)
        return carry

    lax.fori_loop(1, peers, greet, 0)

    @pl.when(s > 0)
    def _():
        pl.semaphore_signal(barrier, inc=1, device_id=(s - 1, d), device_id_type=MESH)

    @pl.when(s < last)
    def _():
        pl.semaphore_signal(barrier, inc=1, device_id=(s + 1, d), device_id_type=MESH)

    pl.semaphore_wait(barrier, peers - 1 + jnp.minimum(s, 1) + jnp.minimum(last - s, 1))

    def spread_rows(dest, m):
        dest[m] = jnp.zeros((ROWS, width), BF)
        dest[m, 0:tokens, :] = xbuf[m]

    @pl.when(s == 0)
    def _():
        load_x.wait()
        for m in range(micros):
            spread_rows(hid, m)

    @pl.when(s == last)
    def _():
        load_g.wait()
        for m in range(micros):
            spread_rows(gout, m)

    def place_of(i):
        pair, inner = i >> 3, i & 7
        far = jnp.where(pair == 0, 3, jnp.where(pair == 1, 4, 4 - pair))
        dz = jnp.where((inner & 1) == 0, far, (5 + pair) & 7)
        rank = inner >> 1
        dy = jnp.where(rank == 0, 2, jnp.where(rank == 1, 1, jnp.where(rank == 2, 3, 0)))
        return dy, dz

    def onward(i):
        dy, dz = place_of(i)
        return (((y + dy) & (NY - 1)) << 3) + ((z + dz) & (NZ - 1))

    def homeward(i):
        dy, dz = place_of(i)
        return (((y - dy) & (NY - 1)) << 3) + ((z - dz) & (NZ - 1))

    def chosen(m):
        ids = [routes[0, m, p // topk, p % topk] for p in range(tokens * topk)]
        found = []
        for p, e in enumerate(ids):
            place = jnp.int32(0)
            for q in range(p):
                place = place + jnp.where(ids[q] == e, 1, 0)
            found.append((p // topk, e * CAP + place, gates[0, m, p // topk, p % topk]))
        return found

    def by_slot(m, weighted):
        count = 2 * slots if weighted else slots
        row = lax.broadcasted_iota(jnp.int32, (count, ROWS), 0)
        col = lax.broadcasted_iota(jnp.int32, (count, ROWS), 1)
        table = jnp.zeros((count, ROWS), F32)
        for t, slot, gate in chosen(m):
            hit = ((row & (slots - 1)) == slot) & (col == t)
            table = jnp.where(hit, gate if weighted else 1.0, table)
        if weighted:
            high = table.astype(BF).astype(F32)
            table = jnp.where(row < slots, high, table - high)
        return table.astype(BF)

    def by_token(m, weighted):
        count = 2 * ROWS if weighted else ROWS
        row = lax.broadcasted_iota(jnp.int32, (count, pairs), 0)
        col = lax.broadcasted_iota(jnp.int32, (count, pairs), 1)
        slot_of = ((onward(col >> 1) >> 2) << 1) + (col & 1)
        table = jnp.zeros((count, pairs), F32)
        for t, slot, gate in chosen(m):
            hit = (slot_of == slot) & ((row & (ROWS - 1)) == t)
            table = jnp.where(hit, gate if weighted else 1.0, table)
        if weighted:
            high = table.astype(BF).astype(F32)
            table = jnp.where(row < ROWS, high, table - high)
        return table.astype(BF)

    def dispatch(send, rows, m, phase):
        def start(i, carry):
            peer = onward(i)
            pltpu.make_async_remote_copy(
                src_ref=send.at[m, :, peer >> 2],
                dst_ref=rows.at[m, :, i],
                send_sem=sent.at[phase, m],
                recv_sem=recv.at[phase, m, i // span],
                device_id=(s, peer),
                device_id_type=MESH,
            ).start()
            return carry

        lax.fori_loop(0, peers - 1, start, 0)
        pltpu.make_async_copy(
            send.at[m, :, d >> 2], rows.at[m, :, peers - 1], recv.at[phase, m, CHUNKS - 1]
        ).start()

    def give_back(out, ret, m, phase, chunk):
        def start(i, carry):
            pltpu.make_async_remote_copy(
                src_ref=out.at[m, :, i],
                dst_ref=ret.at[m, :, i],
                send_sem=sent.at[phase, m],
                recv_sem=recv.at[phase, m, 0],
                device_id=(s, homeward(i)),
                device_id_type=MESH,
            ).start()
            return carry

        final = chunk == CHUNKS - 1
        lax.fori_loop(chunk * span, peers - 1 if final else (chunk + 1) * span, start, 0)
        if final:
            pltpu.make_async_copy(
                out.at[m, :, peers - 1], ret.at[m, :, peers - 1], recv.at[phase, m, 0]
            ).start()

    def arrived(part, sem):
        pltpu.make_async_copy(part, part, sem).wait()

    def flat(buf, m, count, first, size):
        view = buf.at[m].reshape(tiles, count, LANES)
        return jnp.concatenate([view[k, first : first + size, :] for k in range(tiles)], axis=1)

    def store_flat(buf, m, count, first, tile, value):
        view = buf.at[m].reshape(tiles, count, LANES)
        size = value.shape[0]
        for k in range(value.shape[1] // LANES):
            view[tile + k, first : first + size, :] = value[:, k * LANES : (k + 1) * LANES]

    def hop(src, dst, m, way, to):
        return pltpu.make_async_remote_copy(
            src_ref=src.at[m],
            dst_ref=dst.at[m],
            send_sem=hop_sent.at[way, m],
            recv_sem=hop_recv.at[way, m],
            device_id=(to, d),
            device_id_type=MESH,
        )

    def normalize(m):
        values = hid[m].astype(F32)
        inv = lax.rsqrt(jnp.mean(values * values, axis=1, keepdims=True) + norm_eps)
        return values, inv

    def turn_weights():
        for k in range(0, width, WIDE):
            win_t[:, k : k + WIDE] = win[k : k + WIDE, :].T
            wdn_t[k : k + WIDE, :] = wdn[:, k : k + WIDE].T

    def forward_source(m):
        table = by_slot(m, False)

        @pl.when(s > 0)
        def _():
            hop(aout, hid, m, 0, s).wait_recv()

        values, inv = normalize(m)
        normed = (values * inv * gain_ref[...]).astype(BF)
        block = jnp.dot(table, normed, preferred_element_type=F32)
        store_flat(send_f, m, slots, 0, 0, block.astype(BF))
        dispatch(send_f, rows_f, m, 0)

    def forward_expert(m, reply):
        for chunk in range(CHUNKS):
            first, size = chunk * span * CAP, span * CAP
            arrived(rows_f.at[m, :, chunk * span : (chunk + 1) * span], recv.at[0, m, chunk])
            pre = jnp.dot(flat(rows_f, m, pairs, first, size), win[...], preferred_element_type=F32)
            gate, up = pre[:, :units], pre[:, units:]
            sigma = jax.nn.sigmoid(gate)
            inner = (gate * sigma * up).astype(BF)
            for k in range(0, width, WIDE):
                part = jnp.dot(inner, wdn[:, k : k + WIDE], preferred_element_type=F32)
                store_flat(out_f, m, pairs, first, k // LANES, part.astype(BF))
            if reply:
                give_back(out_f, ret_f, m, 1, chunk)
            fac_a[m, first : first + size, :] = up * sigma * (1.0 + gate * (1.0 - sigma))
            fac_b[m, first : first + size, :] = gate * sigma

    def forward_combine(m):
        table = by_token(m, True)
        arrived(ret_f.at[m], recv.at[1, m, 0])
        both = jnp.dot(table, flat(ret_f, m, pairs, 0, pairs), preferred_element_type=F32)
        result = (hid[m].astype(F32) + (both[:ROWS] + both[ROWS:])).astype(BF)
        aout[m] = result

        @pl.when(s < last)
        def _():
            hop(aout, hid, m, 0, s + 1).start()

        acts_ref[0, m] = result[:tokens]

    def backward_source(m):
        table = by_slot(m, True)

        @pl.when(s < last)
        def _():
            hop(bout, gout, m, 1, s).wait_recv()

        block = jnp.dot(table, gout[m], preferred_element_type=F32)
        store_flat(send_b, m, slots, 0, 0, (block[:slots] + block[slots:]).astype(BF))
        dispatch(send_b, rows_b, m, 2)

    def backward_expert(m):
        for chunk in range(CHUNKS):
            first, size = chunk * span * CAP, span * CAP
            arrived(rows_b.at[m, :, chunk * span : (chunk + 1) * span], recv.at[2, m, chunk])
            d_inner = jnp.dot(
                flat(rows_b, m, pairs, first, size), wdn_t[...], preferred_element_type=F32
            )
            d_both = jnp.concatenate(
                [d_inner * fac_a[m, first : first + size, :], d_inner * fac_b[m, first : first + size, :]],
                axis=1,
            ).astype(BF)
            for k in range(0, width, WIDE):
                part = jnp.dot(d_both, win_t[:, k : k + WIDE], preferred_element_type=F32)
                store_flat(out_b, m, pairs, first, k // LANES, part.astype(BF))
            give_back(out_b, ret_b, m, 3, chunk)

    def backward_combine(m):
        values, inv = normalize(m)
        table = by_token(m, False)
        arrived(ret_b.at[m], recv.at[3, m, 0])
        d_normed = jnp.dot(table, flat(ret_b, m, pairs, 0, pairs), preferred_element_type=F32)
        d_scaled = d_normed * gain_ref[...]
        product = jnp.sum(d_scaled * values, axis=1, keepdims=True)
        result = gout[m].astype(F32) + inv * d_scaled - (inv * inv * inv * product / width) * values
        result = result.astype(BF)
        bout[m] = result

        @pl.when(s > 0)
        def _():
            hop(bout, gout, m, 1, s - 1).start()

        grads_ref[0, m] = result[:tokens]

    def each(step):
        def body(m, carry):
            step(m)
            return carry

        lax.fori_loop(0, micros, body, 0)

    def weights_ready():
        load_in.wait()
        load_down.wait()

    @pl.when(s > 0)
    def _():
        weights_ready()
        turn_weights()

    @pl.when(s == last)
    def _():
        each(backward_source)

    forward_source(0)

    @pl.when(s == 0)
    def _():
        weights_ready()

    @pl.when(s < last)
    def _():
        def forward(m):
            forward_expert(m, True)

            @pl.when(m < micros - 1)
            def _():
                forward_source(m + 1)

            forward_combine(m)

        each(forward)

        @pl.when(s == 0)
        def _():
            turn_weights()

        backward_source(0)

        def backward(m):
            backward_expert(m)

            @pl.when(m < micros - 1)
            def _():
                backward_source(m + 1)

            backward_combine(m)

        each(backward)

    @pl.when(s == last)
    def _():
        def turn(m):
            forward_expert(m, False)
            backward_expert(m)

            @pl.when(m < micros - 1)
            def _():
                forward_source(m + 1)

            backward_combine(m)

        each(turn)

        def reply(m):
            for chunk in range(CHUNKS):
                give_back(out_f, ret_f, m, 1, chunk)

        each(reply)
        each(forward_combine)

    def settle(m, carry):
        for phase in range(4):
            most = out_f.at[m, :, 0 : peers - 1]
            pltpu.make_async_copy(most, most, sent.at[phase, m]).wait()

        @pl.when(s < last)
        def _():
            hop(aout, hid, m, 0, s + 1).wait_send()

        @pl.when(s > 0)
        def _():
            hop(bout, gout, m, 1, s - 1).wait_send()

        return carry

    lax.fori_loop(0, micros, settle, 0)


def local(x_in, grad_in, norm_gain, w_in, w_down, routes, gates):
    peers = lax.axis_size("expert")
    micros, tokens, width = x_in.shape
    cols = w_in.shape[2]
    units = w_down.shape[1]
    tiles = width // LANES
    out = jax.ShapeDtypeStruct((1, micros, tokens, width), BF)
    small = pltpu.VMEM((micros, tiles, peers // GROUP, CAP, LANES), BF)
    large = pltpu.VMEM((micros, tiles, peers, CAP, LANES), BF)
    state = pltpu.VMEM((micros, ROWS, width), BF)
    factor = pltpu.VMEM((micros, peers * CAP, units), F32)
    anywhere = pl.BlockSpec(memory_space=pl.ANY)
    vmem = pl.BlockSpec(memory_space=pltpu.VMEM)
    smem = pl.BlockSpec(memory_space=pltpu.SMEM)
    return pl.pallas_call(
        layer_kernel,
        out_shape=(out, out),
        in_specs=[anywhere, anywhere, vmem, anywhere, anywhere, smem, smem],
        out_specs=(vmem, vmem),
        scratch_shapes=[
            pltpu.VMEM((width, cols), BF),
            pltpu.VMEM((units, width), BF),
            pltpu.VMEM((cols, width), BF),
            pltpu.VMEM((width, units), BF),
            pltpu.VMEM((micros, tokens, width), BF),
            state, state, state, state,
            small, large, large, large,
            small, large, large, large,
            factor, factor,
            pltpu.SemaphoreType.DMA((2,)),
            pltpu.SemaphoreType.DMA,
            pltpu.SemaphoreType.DMA((4, micros, CHUNKS)),
            pltpu.SemaphoreType.DMA((4, micros)),
            pltpu.SemaphoreType.DMA((2, micros)),
            pltpu.SemaphoreType.DMA((2, micros)),
        ],
        compiler_params=pltpu.CompilerParams(
            collective_id=0, has_side_effects=True, vmem_limit_bytes=56 << 20
        ),
    )(x_in, grad_in, norm_gain, w_in, w_down, routes, gates)


def solution(mesh):
    placed = (
        P(None, "expert", None),
        P(None, "expert", None),
        P("pipe", None),
        P("pipe", None, "expert"),
        P("pipe", "expert", None),
        P("pipe", None, "expert", None),
        P("pipe", None, "expert", None),
    )
    return jax.shard_map(
        local,
        mesh=mesh,
        in_specs=placed,
        out_specs=(P("pipe", None, "expert", None), P("pipe", None, "expert", None)),
        check_vma=False,
    )
```

```python
import jax
import jax.numpy as jnp
from jax import lax
from jax.experimental import pallas as pl
from jax.experimental.pallas import tpu as pltpu
from jax.sharding import PartitionSpec as P

MESH = pl.DeviceIdType.MESH
GROUP = 4
CAP = 2
LANES = 128
ROWS = 8
WIDE = 512
NY = 4
NZ = 8
CHUNKS = 4
EARLY = 1
norm_eps = 1e-06
BF = jnp.bfloat16
F32 = jnp.float32


def layer_kernel(
    x_hbm, gin_hbm, gain_ref, win_hbm, wdn_hbm, routes, gates,
    acts_ref, grads_ref,
    win, wdn, win_t, wdn_t, xbuf, hid, gout, aout, bout,
    send_f, rows_f, out_f, ret_f, send_b, rows_b, out_b, ret_b, fac_a, fac_b,
    wsem, xsem, recv, sent, hop_recv, hop_sent,
):
    sections = lax.axis_size("pipe")
    peers = lax.axis_size("expert")
    s = lax.axis_index("pipe")
    d = lax.axis_index("expert")
    tokens, micros, width = xbuf.shape
    topk = routes.shape[2]
    units = wdn.shape[0]
    tiles = width // LANES
    slots = send_f.shape[2] * CAP
    pairs = peers * CAP
    last = sections - 1
    span = peers // CHUNKS
    y, z = d >> 3, d & (NZ - 1)

    load_in = pltpu.make_async_copy(win_hbm.at[0], win, wsem.at[0])
    load_down = pltpu.make_async_copy(wdn_hbm.at[0], wdn, wsem.at[1])
    load_x = pltpu.make_async_copy(x_hbm, xbuf, xsem)
    load_g = pltpu.make_async_copy(gin_hbm, xbuf, xsem)

    @pl.when(s == 0)
    def _():
        load_x.start()

    @pl.when(s == last)
    def _():
        load_g.start()

    load_in.start()
    load_down.start()

    barrier = pltpu.get_barrier_semaphore()

    def greet(i, carry):
        pl.semaphore_signal(barrier, inc=1, device_id=(s, lax.rem(d + i, peers)), device_id_type=MESH)
        return carry

    lax.fori_loop(1, peers, greet, 0)

    @pl.when(s > 0)
    def _():
        pl.semaphore_signal(barrier, inc=1, device_id=(s - 1, d), device_id_type=MESH)

    @pl.when(s < last)
    def _():
        pl.semaphore_signal(barrier, inc=1, device_id=(s + 1, d), device_id_type=MESH)

    pl.semaphore_wait(barrier, peers - 1 + jnp.minimum(s, 1) + jnp.minimum(last - s, 1))

    def spread_rows(dest, m):
        dest[m] = jnp.zeros((ROWS, width), BF)
        dest[m, 0:tokens, :] = xbuf[:, m, :]

    @pl.when(s == 0)
    def _():
        load_x.wait()
        for m in range(micros):
            spread_rows(hid, m)

    @pl.when(s == last)
    def _():
        load_g.wait()
        for m in range(micros):
            spread_rows(gout, m)

    def place_of(i):
        pair, inner = i >> 3, i & 7
        far = jnp.where(pair == 0, 3, jnp.where(pair == 1, 4, 4 - pair))
        dz = jnp.where((inner & 1) == 0, far, (5 + pair) & 7)
        rank = inner >> 1
        dy = jnp.where(rank == 0, 2, jnp.where(rank == 1, 1, jnp.where(rank == 2, 3, 0)))
        return dy, dz

    def onward(i):
        dy, dz = place_of(i)
        return (((y + dy) & (NY - 1)) << 3) + ((z + dz) & (NZ - 1))

    def homeward(i):
        dy, dz = place_of(i)
        return (((y - dy) & (NY - 1)) << 3) + ((z - dz) & (NZ - 1))

    def chosen(m):
        ids = [routes[0, m, p % topk, p // topk] for p in range(tokens * topk)]
        found = []
        for p, e in enumerate(ids):
            place = jnp.int32(0)
            for q in range(p):
                place = place + jnp.where(ids[q] == e, 1, 0)
            found.append((p // topk, e * CAP + place, gates[0, m, p % topk, p // topk]))
        return found

    def by_slot(m, weighted):
        count = 2 * slots if weighted else slots
        row = lax.broadcasted_iota(jnp.int32, (count, ROWS), 0)
        col = lax.broadcasted_iota(jnp.int32, (count, ROWS), 1)
        table = jnp.zeros((count, ROWS), F32)
        for t, slot, gate in chosen(m):
            hit = ((row & (slots - 1)) == slot) & (col == t)
            table = jnp.where(hit, gate if weighted else 1.0, table)
        if weighted:
            high = table.astype(BF).astype(F32)
            table = jnp.where(row < slots, high, table - high)
        return table.astype(BF)

    def by_token(m, weighted):
        count = 2 * ROWS if weighted else ROWS
        row = lax.broadcasted_iota(jnp.int32, (count, pairs), 0)
        col = lax.broadcasted_iota(jnp.int32, (count, pairs), 1)
        slot_of = ((onward(col >> 1) >> 2) << 1) + (col & 1)
        table = jnp.zeros((count, pairs), F32)
        for t, slot, gate in chosen(m):
            hit = (slot_of == slot) & ((row & (ROWS - 1)) == t)
            table = jnp.where(hit, gate if weighted else 1.0, table)
        if weighted:
            high = table.astype(BF).astype(F32)
            table = jnp.where(row < ROWS, high, table - high)
        return table.astype(BF)

    def dispatch(send, rows, m, phase):
        def start(i, carry):
            peer = onward(i)
            pltpu.make_async_remote_copy(
                src_ref=send.at[m, :, peer >> 2],
                dst_ref=rows.at[m, :, i],
                send_sem=sent.at[phase, m],
                recv_sem=recv.at[phase, m, i // span],
                device_id=(s, peer),
                device_id_type=MESH,
            ).start()
            return carry

        lax.fori_loop(0, peers - 1, start, 0)
        pltpu.make_async_copy(
            send.at[m, :, d >> 2], rows.at[m, :, peers - 1], recv.at[phase, m, CHUNKS - 1]
        ).start()

    def give_back(out, ret, m, phase, chunk):
        def start(i, carry):
            pltpu.make_async_remote_copy(
                src_ref=out.at[m, :, i],
                dst_ref=ret.at[m, :, i],
                send_sem=sent.at[phase, m],
                recv_sem=recv.at[phase, m, 0],
                device_id=(s, homeward(i)),
                device_id_type=MESH,
            ).start()
            return carry

        final = chunk == CHUNKS - 1
        lax.fori_loop(chunk * span, peers - 1 if final else (chunk + 1) * span, start, 0)
        if final:
            pltpu.make_async_copy(
                out.at[m, :, peers - 1], ret.at[m, :, peers - 1], recv.at[phase, m, 0]
            ).start()

    def arrived(part, sem):
        pltpu.make_async_copy(part, part, sem).wait()

    def flat(buf, m, count, first, size):
        view = buf.at[m].reshape(tiles, count, LANES)
        return jnp.concatenate([view[k, first : first + size, :] for k in range(tiles)], axis=1)

    def store_flat(buf, m, count, first, tile, value):
        view = buf.at[m].reshape(tiles, count, LANES)
        size = value.shape[0]
        for k in range(value.shape[1] // LANES):
            view[tile + k, first : first + size, :] = value[:, k * LANES : (k + 1) * LANES]

    def hop(src, dst, m, way, to):
        return pltpu.make_async_remote_copy(
            src_ref=src.at[m],
            dst_ref=dst.at[m],
            send_sem=hop_sent.at[way, m],
            recv_sem=hop_recv.at[way, m],
            device_id=(to, d),
            device_id_type=MESH,
        )

    def normalize(m):
        values = hid[m].astype(F32)
        inv = lax.rsqrt(jnp.mean(values * values, axis=1, keepdims=True) + norm_eps)
        return values, inv

    def turn_weights():
        for k in range(0, width, WIDE):
            win_t[:, k : k + WIDE] = win[k : k + WIDE, :].T
            wdn_t[k : k + WIDE, :] = wdn[:, k : k + WIDE].T

    def forward_source(m):
        table = by_slot(m, False)

        @pl.when(s > 0)
        def _():
            hop(aout, hid, m, 0, s).wait_recv()

        values, inv = normalize(m)
        normed = (values * inv * gain_ref[...]).astype(BF)
        block = jnp.dot(table, normed, preferred_element_type=F32)
        store_flat(send_f, m, slots, 0, 0, block.astype(BF))
        dispatch(send_f, rows_f, m, 0)

    def forward_expert(m):
        for chunk in range(CHUNKS):
            first, size = chunk * span * CAP, span * CAP
            arrived(rows_f.at[m, :, chunk * span : (chunk + 1) * span], recv.at[0, m, chunk])
            pre = jnp.dot(flat(rows_f, m, pairs, first, size), win[...], preferred_element_type=F32)
            gate, up = pre[:, :units], pre[:, units:]
            sigma = jax.nn.sigmoid(gate)
            inner = (gate * sigma * up).astype(BF)
            for k in range(0, width, WIDE):
                part = jnp.dot(inner, wdn[:, k : k + WIDE], preferred_element_type=F32)
                store_flat(out_f, m, pairs, first, k // LANES, part.astype(BF))

            @pl.when(s < last)
            def _():
                give_back(out_f, ret_f, m, 1, chunk)

            fac_a[m, first : first + size, :] = up * sigma * (1.0 + gate * (1.0 - sigma))
            fac_b[m, first : first + size, :] = gate * sigma

    def forward_combine(m):
        table = by_token(m, True)
        arrived(ret_f.at[m], recv.at[1, m, 0])
        both = jnp.dot(table, flat(ret_f, m, pairs, 0, pairs), preferred_element_type=F32)
        result = (hid[m].astype(F32) + (both[:ROWS] + both[ROWS:])).astype(BF)
        aout[m] = result

        @pl.when(s < last)
        def _():
            hop(aout, hid, m, 0, s + 1).start()


    def backward_source(m):
        table = by_slot(m, True)

        @pl.when(s < last)
        def _():
            hop(bout, gout, m, 1, s).wait_recv()

        block = jnp.dot(table, gout[m], preferred_element_type=F32)
        store_flat(send_b, m, slots, 0, 0, (block[:slots] + block[slots:]).astype(BF))
        dispatch(send_b, rows_b, m, 2)

    def backward_expert(m):
        for chunk in range(CHUNKS):
            first, size = chunk * span * CAP, span * CAP
            arrived(rows_b.at[m, :, chunk * span : (chunk + 1) * span], recv.at[2, m, chunk])
            d_inner = jnp.dot(
                flat(rows_b, m, pairs, first, size), wdn_t[...], preferred_element_type=F32
            )
            d_both = jnp.concatenate(
                [d_inner * fac_a[m, first : first + size, :], d_inner * fac_b[m, first : first + size, :]],
                axis=1,
            ).astype(BF)
            for k in range(0, width, WIDE):
                part = jnp.dot(d_both, win_t[:, k : k + WIDE], preferred_element_type=F32)
                store_flat(out_b, m, pairs, first, k // LANES, part.astype(BF))
            give_back(out_b, ret_b, m, 3, chunk)

    def backward_combine(m):
        values, inv = normalize(m)
        table = by_token(m, False)
        arrived(ret_b.at[m], recv.at[3, m, 0])
        d_normed = jnp.dot(table, flat(ret_b, m, pairs, 0, pairs), preferred_element_type=F32)
        d_scaled = d_normed * gain_ref[...]
        product = jnp.sum(d_scaled * values, axis=1, keepdims=True)
        result = gout[m].astype(F32) + inv * d_scaled - (inv * inv * inv * product / width) * values
        result = result.astype(BF)
        bout[m] = result

        @pl.when(s > 0)
        def _():
            hop(bout, gout, m, 1, s - 1).start()


    def each(step):
        def body(m, carry):
            step(m)
            return carry

        lax.fori_loop(0, micros, body, 0)

    def weights_ready():
        load_in.wait()
        load_down.wait()

    @pl.when(s > 0)
    def _():
        weights_ready()
        turn_weights()

    @pl.when(s == last)
    def _():
        each(backward_source)

    lag = jnp.minimum(2 * (last - s), micros)
    early = s < EARLY

    @pl.when(s == 0)
    def _():
        forward_source(0)
        weights_ready()

    def tick(k, carry):
        ahead, behind = k < micros, k >= lag

        @pl.when(ahead & ((s > 0) & jnp.logical_not(early & (k > 0)) | (s == 0) & (k > 0) & jnp.logical_not(early)))
        def _():
            forward_source(k)

        @pl.when(behind & (s < last))
        def _():
            backward_source(k - lag)

        @pl.when(ahead)
        def _():
            forward_expert(k)

        @pl.when(early & (k + 1 < micros))
        def _():
            forward_source(k + 1)

        @pl.when(behind)
        def _():
            backward_expert(k - lag)

        @pl.when(ahead & (s < last))
        def _():
            forward_combine(k)

        @pl.when((s == 0) & (k == micros - 1))
        def _():
            turn_weights()

        @pl.when(behind)
        def _():
            backward_combine(k - lag)

        return carry

    lax.fori_loop(0, micros + lag, tick, 0)

    @pl.when(s == last)
    def _():
        def reply(m):
            for chunk in range(CHUNKS):
                give_back(out_f, ret_f, m, 1, chunk)

        each(reply)
        each(forward_combine)

    for m in range(micros):
        acts_ref[0, :, m, :] = aout[m, 0:tokens, :]
        grads_ref[0, :, m, :] = bout[m, 0:tokens, :]

    def settle(m, carry):
        for phase in range(4):
            most = out_f.at[m, :, 0 : peers - 1]
            pltpu.make_async_copy(most, most, sent.at[phase, m]).wait()

        @pl.when(s < last)
        def _():
            hop(aout, hid, m, 0, s + 1).wait_send()

        @pl.when(s > 0)
        def _():
            hop(bout, gout, m, 1, s - 1).wait_send()

        return carry

    lax.fori_loop(0, micros, settle, 0)


def local(x_in, grad_in, norm_gain, w_in, w_down, routes, gates):
    peers = lax.axis_size("expert")
    micros, tokens, width = x_in.shape
    cols = w_in.shape[2]
    units = w_down.shape[1]
    tiles = width // LANES
    out = jax.ShapeDtypeStruct((1, tokens, micros, width), BF)
    small = pltpu.VMEM((micros, tiles, peers // GROUP, CAP, LANES), BF)
    large = pltpu.VMEM((micros, tiles, peers, CAP, LANES), BF)
    state = pltpu.VMEM((micros, ROWS, width), BF)
    factor = pltpu.VMEM((micros, peers * CAP, units), F32)
    anywhere = pl.BlockSpec(memory_space=pl.ANY)
    vmem = pl.BlockSpec(memory_space=pltpu.VMEM)
    smem = pl.BlockSpec(memory_space=pltpu.SMEM)
    acts, grads = pl.pallas_call(
        layer_kernel,
        out_shape=(out, out),
        in_specs=[anywhere, anywhere, vmem, anywhere, anywhere, smem, smem],
        out_specs=(vmem, vmem),
        scratch_shapes=[
            pltpu.VMEM((width, cols), BF),
            pltpu.VMEM((units, width), BF),
            pltpu.VMEM((cols, width), BF),
            pltpu.VMEM((width, units), BF),
            pltpu.VMEM((tokens, micros, width), BF),
            state, state, state, state,
            small, large, large, large,
            small, large, large, large,
            factor, factor,
            pltpu.SemaphoreType.DMA((2,)),
            pltpu.SemaphoreType.DMA,
            pltpu.SemaphoreType.DMA((4, micros, CHUNKS)),
            pltpu.SemaphoreType.DMA((4, micros)),
            pltpu.SemaphoreType.DMA((2, micros)),
            pltpu.SemaphoreType.DMA((2, micros)),
        ],
        compiler_params=pltpu.CompilerParams(
            collective_id=0, has_side_effects=True, vmem_limit_bytes=56 << 20
        ),
    )(
        jnp.swapaxes(x_in, 0, 1),
        jnp.swapaxes(grad_in, 0, 1),
        norm_gain,
        w_in,
        w_down,
        jnp.swapaxes(routes, 2, 3),
        jnp.swapaxes(gates, 2, 3),
    )
    return jnp.swapaxes(acts, 1, 2), jnp.swapaxes(grads, 1, 2)


def solution(mesh):
    placed = (
        P(None, "expert", None),
        P(None, "expert", None),
        P("pipe", None),
        P("pipe", None, "expert"),
        P("pipe", "expert", None),
        P("pipe", None, "expert", None),
        P("pipe", None, "expert", None),
    )
    return jax.shard_map(
        local,
        mesh=mesh,
        in_specs=placed,
        out_specs=(P("pipe", None, "expert", None), P("pipe", None, "expert", None)),
        check_vma=False,
    )
```

```python
import jax
import jax.numpy as jnp
from jax import lax
from jax.experimental import pallas as pl
from jax.experimental.pallas import tpu as pltpu
from jax.sharding import PartitionSpec as P

MESH = pl.DeviceIdType.MESH
GROUP = 4
CAP = 2
LANES = 128
ROWS = 8
WIDE = 512
NY = 4
NZ = 8
CHUNKS = 4
OWN = 15
EARLY = 1
norm_eps = 1e-06
BF = jnp.bfloat16
F32 = jnp.float32


def layer_kernel(
    x_hbm, gin_hbm, gain_ref, win_hbm, wdn_hbm, routes, gates,
    acts_ref, grads_ref,
    win, wdn, win_t, wdn_t, xbuf, hid, gout, aout, bout,
    send_f, rows_f, out_f, ret_f, send_b, rows_b, out_b, ret_b, fac_a, fac_b,
    wsem, xsem, recv, sent, hop_recv, hop_sent,
):
    sections = lax.axis_size("pipe")
    peers = lax.axis_size("expert")
    s = lax.axis_index("pipe")
    d = lax.axis_index("expert")
    tokens, micros, width = xbuf.shape
    topk = routes.shape[2]
    units = wdn.shape[0]
    tiles = width // LANES
    slots = send_f.shape[2] * CAP
    pairs = peers * CAP
    last = sections - 1
    span = peers // CHUNKS
    y, z = d >> 3, d & (NZ - 1)

    load_in = pltpu.make_async_copy(win_hbm.at[0], win, wsem.at[0])
    load_down = pltpu.make_async_copy(wdn_hbm.at[0], wdn, wsem.at[1])
    load_x = pltpu.make_async_copy(x_hbm, xbuf, xsem)
    load_g = pltpu.make_async_copy(gin_hbm, xbuf, xsem)

    @pl.when(s == 0)
    def _():
        load_x.start()

    @pl.when(s == last)
    def _():
        load_g.start()

    load_in.start()
    load_down.start()

    barrier = pltpu.get_barrier_semaphore()

    def greet(i, carry):
        pl.semaphore_signal(barrier, inc=1, device_id=(s, lax.rem(d + i, peers)), device_id_type=MESH)
        return carry

    lax.fori_loop(1, peers, greet, 0)

    @pl.when(s > 0)
    def _():
        pl.semaphore_signal(barrier, inc=1, device_id=(s - 1, d), device_id_type=MESH)

    @pl.when(s < last)
    def _():
        pl.semaphore_signal(barrier, inc=1, device_id=(s + 1, d), device_id_type=MESH)

    pl.semaphore_wait(barrier, peers - 1 + jnp.minimum(s, 1) + jnp.minimum(last - s, 1))

    def spread_rows(dest, m):
        dest[m] = jnp.zeros((ROWS, width), BF)
        dest[m, 0:tokens, :] = xbuf[:, m, :]

    @pl.when(s == 0)
    def _():
        load_x.wait()
        for m in range(micros):
            spread_rows(hid, m)

    @pl.when(s == last)
    def _():
        load_g.wait()
        for m in range(micros):
            spread_rows(gout, m)

    def place_of(i):
        pair, inner = i >> 3, i & 7
        far = jnp.where(pair == 0, 3, jnp.where(pair == 1, 4, 4 - pair))
        near = jnp.where(pair == 0, 5, jnp.where(pair == 1, 0, 4 + pair))
        dz = jnp.where((inner & 1) == 0, far, near)
        rank = inner >> 1
        dy = jnp.where(rank == 0, 2, jnp.where(rank == 1, 1, jnp.where(rank == 2, 3, 0)))
        return dy, dz

    def onward(i):
        dy, dz = place_of(i)
        return (((y + dy) & (NY - 1)) << 3) + ((z + dz) & (NZ - 1))

    def homeward(i):
        dy, dz = place_of(i)
        return (((y - dy) & (NY - 1)) << 3) + ((z - dz) & (NZ - 1))

    def chosen(m):
        ids = [routes[0, m, p % topk, p // topk] for p in range(tokens * topk)]
        found = []
        for p, e in enumerate(ids):
            place = jnp.int32(0)
            for q in range(p):
                place = place + jnp.where(ids[q] == e, 1, 0)
            found.append((p // topk, e * CAP + place, gates[0, m, p % topk, p // topk]))
        return found

    def by_slot(m, weighted):
        count = 2 * slots if weighted else slots
        row = lax.broadcasted_iota(jnp.int32, (count, ROWS), 0)
        col = lax.broadcasted_iota(jnp.int32, (count, ROWS), 1)
        table = jnp.zeros((count, ROWS), F32)
        for t, slot, gate in chosen(m):
            hit = ((row & (slots - 1)) == slot) & (col == t)
            table = jnp.where(hit, gate if weighted else 1.0, table)
        if weighted:
            high = table.astype(BF).astype(F32)
            table = jnp.where(row < slots, high, table - high)
        return table.astype(BF)

    def by_token(m, weighted):
        count = 2 * ROWS if weighted else ROWS
        row = lax.broadcasted_iota(jnp.int32, (count, pairs), 0)
        col = lax.broadcasted_iota(jnp.int32, (count, pairs), 1)
        slot_of = ((onward(col >> 1) >> 2) << 1) + (col & 1)
        table = jnp.zeros((count, pairs), F32)
        for t, slot, gate in chosen(m):
            hit = (slot_of == slot) & ((row & (ROWS - 1)) == t)
            table = jnp.where(hit, gate if weighted else 1.0, table)
        if weighted:
            high = table.astype(BF).astype(F32)
            table = jnp.where(row < ROWS, high, table - high)
        return table.astype(BF)

    def dispatch(send, rows, m, phase):
        def start(j, carry):
            i = j + jnp.where(j >= OWN, 1, 0)
            peer = onward(i)
            pltpu.make_async_remote_copy(
                src_ref=send.at[m, :, peer >> 2],
                dst_ref=rows.at[m, :, i],
                send_sem=sent.at[phase, m],
                recv_sem=recv.at[phase, m, i // span],
                device_id=(s, peer),
                device_id_type=MESH,
            ).start()
            return carry

        lax.fori_loop(0, peers - 1, start, 0)
        pltpu.make_async_copy(
            send.at[m, :, d >> 2], rows.at[m, :, OWN], recv.at[phase, m, OWN // span]
        ).start()

    def give_back(out, ret, m, phase, chunk):
        def start(j, carry):
            i = j + jnp.where(j >= OWN, 1, 0)
            pltpu.make_async_remote_copy(
                src_ref=out.at[m, :, i],
                dst_ref=ret.at[m, :, i],
                send_sem=sent.at[phase, m],
                recv_sem=recv.at[phase, m, 0],
                device_id=(s, homeward(i)),
                device_id_type=MESH,
            ).start()
            return carry

        own = OWN // span
        first = chunk * span - jnp.where(chunk > own, 1, 0)
        end = (chunk + 1) * span - jnp.where(chunk >= own, 1, 0)
        lax.fori_loop(first, end, start, 0)

        @pl.when(chunk == own)
        def _():
            pltpu.make_async_copy(
                out.at[m, :, OWN], ret.at[m, :, OWN], recv.at[phase, m, 0]
            ).start()

    def arrived(part, sem):
        pltpu.make_async_copy(part, part, sem).wait()

    def flat(buf, m, count, first, size):
        view = buf.at[m].reshape(tiles, count, LANES)
        return jnp.concatenate([view[k, pl.ds(first, size), :] for k in range(tiles)], axis=1)

    def store_flat(buf, m, count, first, tile, value):
        view = buf.at[m].reshape(tiles, count, LANES)
        size = value.shape[0]
        for k in range(value.shape[1] // LANES):
            view[tile + k, pl.ds(first, size), :] = value[:, k * LANES : (k + 1) * LANES]

    def hop(src, dst, m, way, to):
        return pltpu.make_async_remote_copy(
            src_ref=src.at[m],
            dst_ref=dst.at[m],
            send_sem=hop_sent.at[way, m],
            recv_sem=hop_recv.at[way, m],
            device_id=(to, d),
            device_id_type=MESH,
        )

    def normalize(m):
        values = hid[m].astype(F32)
        inv = lax.rsqrt(jnp.mean(values * values, axis=1, keepdims=True) + norm_eps)
        return values, inv

    def turn_weights():
        for k in range(0, width, WIDE):
            win_t[:, k : k + WIDE] = win[k : k + WIDE, :].T
            wdn_t[k : k + WIDE, :] = wdn[:, k : k + WIDE].T

    def forward_source(m):
        table = by_slot(m, False)

        @pl.when(s > 0)
        def _():
            hop(aout, hid, m, 0, s).wait_recv()

        values, inv = normalize(m)
        normed = (values * inv * gain_ref[...]).astype(BF)
        block = jnp.dot(table, normed, preferred_element_type=F32)
        store_flat(send_f, m, slots, 0, 0, block.astype(BF))
        dispatch(send_f, rows_f, m, 0)

    def forward_chunk(m, chunk):
        size = span * CAP
        first = pl.multiple_of(chunk * size, size)
        arrived(rows_f.at[m, :, pl.ds(chunk * span, span)], recv.at[0, m, chunk])
        pre = jnp.dot(flat(rows_f, m, pairs, first, size), win[...], preferred_element_type=F32)
        gate, up = pre[:, :units], pre[:, units:]
        sigma = jax.nn.sigmoid(gate)
        inner = (gate * sigma * up).astype(BF)
        for k in range(0, width, WIDE):
            part = jnp.dot(inner, wdn[:, k : k + WIDE], preferred_element_type=F32)
            store_flat(out_f, m, pairs, first, k // LANES, part.astype(BF))

        @pl.when(s < last)
        def _():
            give_back(out_f, ret_f, m, 1, chunk)

        fac_a[m, pl.ds(first, size), :] = up * sigma * (1.0 + gate * (1.0 - sigma))
        fac_b[m, pl.ds(first, size), :] = gate * sigma

    def forward_combine(m):
        table = by_token(m, True)
        arrived(ret_f.at[m], recv.at[1, m, 0])
        both = jnp.dot(table, flat(ret_f, m, pairs, 0, pairs), preferred_element_type=F32)
        result = (hid[m].astype(F32) + (both[:ROWS] + both[ROWS:])).astype(BF)
        aout[m] = result

        @pl.when(s < last)
        def _():
            hop(aout, hid, m, 0, s + 1).start()


    def backward_source(m):
        table = by_slot(m, True)

        @pl.when(s < last)
        def _():
            hop(bout, gout, m, 1, s).wait_recv()

        block = jnp.dot(table, gout[m], preferred_element_type=F32)
        store_flat(send_b, m, slots, 0, 0, (block[:slots] + block[slots:]).astype(BF))
        dispatch(send_b, rows_b, m, 2)

    def backward_chunk(m, chunk):
        size = span * CAP
        first = pl.multiple_of(chunk * size, size)
        arrived(rows_b.at[m, :, pl.ds(chunk * span, span)], recv.at[2, m, chunk])
        d_inner = jnp.dot(
            flat(rows_b, m, pairs, first, size), wdn_t[...], preferred_element_type=F32
        )
        d_both = jnp.concatenate(
            [d_inner * fac_a[m, pl.ds(first, size), :], d_inner * fac_b[m, pl.ds(first, size), :]],
            axis=1,
        ).astype(BF)
        for k in range(0, width, WIDE):
            part = jnp.dot(d_both, win_t[:, k : k + WIDE], preferred_element_type=F32)
            store_flat(out_b, m, pairs, first, k // LANES, part.astype(BF))
        give_back(out_b, ret_b, m, 3, chunk)

    def backward_combine(m):
        values, inv = normalize(m)
        table = by_token(m, False)
        arrived(ret_b.at[m], recv.at[3, m, 0])
        d_normed = jnp.dot(table, flat(ret_b, m, pairs, 0, pairs), preferred_element_type=F32)
        d_scaled = d_normed * gain_ref[...]
        product = jnp.sum(d_scaled * values, axis=1, keepdims=True)
        result = gout[m].astype(F32) + inv * d_scaled - (inv * inv * inv * product / width) * values
        result = result.astype(BF)
        bout[m] = result

        @pl.when(s > 0)
        def _():
            hop(bout, gout, m, 1, s - 1).start()


    def each_chunk(step):
        def body(chunk, carry):
            step(chunk)
            return carry

        lax.fori_loop(0, CHUNKS, body, 0)

    def each(step):
        def body(m, carry):
            step(m)
            return carry

        lax.fori_loop(0, micros, body, 0)

    def weights_ready():
        load_in.wait()
        load_down.wait()

    @pl.when(s > 0)
    def _():
        weights_ready()
        turn_weights()

    @pl.when(s == last)
    def _():
        each(backward_source)

    lag = jnp.minimum(2 * (last - s), micros)
    early = s < EARLY

    @pl.when(s == 0)
    def _():
        forward_source(0)
        weights_ready()

    def tick(k, carry):
        ahead, behind = k < micros, k >= lag

        @pl.when(ahead & ((s > 0) & jnp.logical_not(early & (k > 0)) | (s == 0) & (k > 0) & jnp.logical_not(early)))
        def _():
            forward_source(k)

        @pl.when(behind & (s < last))
        def _():
            backward_source(k - lag)

        @pl.when(ahead)
        def _():
            def both_ways(chunk):
                forward_chunk(k, chunk)

                @pl.when(s == last)
                def _():
                    backward_chunk(k, chunk)

            each_chunk(both_ways)

        @pl.when(early & (k + 1 < micros))
        def _():
            forward_source(k + 1)

        @pl.when(behind & (s < last))
        def _():
            each_chunk(lambda chunk: backward_chunk(k - lag, chunk))

        @pl.when(ahead & (s < last))
        def _():
            forward_combine(k)

        @pl.when((s == 0) & (k == micros - 1))
        def _():
            turn_weights()

        @pl.when(behind)
        def _():
            backward_combine(k - lag)

        return carry

    lax.fori_loop(0, micros + lag, tick, 0)

    @pl.when(s == last)
    def _():
        def reply(m):
            each_chunk(lambda chunk: give_back(out_f, ret_f, m, 1, chunk))

        each(reply)
        each(forward_combine)

    for m in range(micros):
        acts_ref[0, :, m, :] = aout[m, 0:tokens, :]
        grads_ref[0, :, m, :] = bout[m, 0:tokens, :]

    def settle(m, carry):
        for phase in range(4):
            most = out_f.at[m, :, 0 : peers - 1]
            pltpu.make_async_copy(most, most, sent.at[phase, m]).wait()

        @pl.when(s < last)
        def _():
            hop(aout, hid, m, 0, s + 1).wait_send()

        @pl.when(s > 0)
        def _():
            hop(bout, gout, m, 1, s - 1).wait_send()

        return carry

    lax.fori_loop(0, micros, settle, 0)


def local(x_in, grad_in, norm_gain, w_in, w_down, routes, gates):
    peers = lax.axis_size("expert")
    micros, tokens, width = x_in.shape
    cols = w_in.shape[2]
    units = w_down.shape[1]
    tiles = width // LANES
    out = jax.ShapeDtypeStruct((1, tokens, micros, width), BF)
    small = pltpu.VMEM((micros, tiles, peers // GROUP, CAP, LANES), BF)
    large = pltpu.VMEM((micros, tiles, peers, CAP, LANES), BF)
    state = pltpu.VMEM((micros, ROWS, width), BF)
    factor = pltpu.VMEM((micros, peers * CAP, units), F32)
    anywhere = pl.BlockSpec(memory_space=pl.ANY)
    vmem = pl.BlockSpec(memory_space=pltpu.VMEM)
    smem = pl.BlockSpec(memory_space=pltpu.SMEM)
    acts, grads = pl.pallas_call(
        layer_kernel,
        out_shape=(out, out),
        in_specs=[anywhere, anywhere, vmem, anywhere, anywhere, smem, smem],
        out_specs=(vmem, vmem),
        scratch_shapes=[
            pltpu.VMEM((width, cols), BF),
            pltpu.VMEM((units, width), BF),
            pltpu.VMEM((cols, width), BF),
            pltpu.VMEM((width, units), BF),
            pltpu.VMEM((tokens, micros, width), BF),
            state, state, state, state,
            small, large, large, large,
            small, large, large, large,
            factor, factor,
            pltpu.SemaphoreType.DMA((2,)),
            pltpu.SemaphoreType.DMA,
            pltpu.SemaphoreType.DMA((4, micros, CHUNKS)),
            pltpu.SemaphoreType.DMA((4, micros)),
            pltpu.SemaphoreType.DMA((2, micros)),
            pltpu.SemaphoreType.DMA((2, micros)),
        ],
        compiler_params=pltpu.CompilerParams(
            collective_id=0, has_side_effects=True, vmem_limit_bytes=56 << 20
        ),
    )(
        jnp.swapaxes(x_in, 0, 1),
        jnp.swapaxes(grad_in, 0, 1),
        norm_gain,
        w_in,
        w_down,
        jnp.swapaxes(routes, 2, 3),
        jnp.swapaxes(gates, 2, 3),
    )
    return jnp.swapaxes(acts, 1, 2), jnp.swapaxes(grads, 1, 2)


def solution(mesh):
    placed = (
        P(None, "expert", None),
        P(None, "expert", None),
        P("pipe", None),
        P("pipe", None, "expert"),
        P("pipe", "expert", None),
        P("pipe", None, "expert", None),
        P("pipe", None, "expert", None),
    )
    return jax.shard_map(
        local,
        mesh=mesh,
        in_specs=placed,
        out_specs=(P("pipe", None, "expert", None), P("pipe", None, "expert", None)),
        check_vma=False,
    )
```

```python
import jax
import jax.numpy as jnp
from jax import lax
from jax.experimental import pallas as pl
from jax.experimental.pallas import tpu as pltpu
from jax.sharding import PartitionSpec as P

MESH = pl.DeviceIdType.MESH
GROUP = 4
CAP = 2
LANES = 128
ROWS = 8
WIDE = 512
NY = 4
NZ = 8
CHUNKS = 4
OWN = 15
EARLY = 1
norm_eps = 1e-06
BF = jnp.bfloat16
F32 = jnp.float32


def layer_kernel(
    x_hbm, gin_hbm, gain_ref, win_hbm, wdn_hbm, routes, gates,
    acts_ref, grads_ref,
    win, wdn, win_t, wdn_t, xbuf, hid, gout, aout, bout,
    send_f, rows_f, out_f, ret_f, send_b, rows_b, out_b, ret_b, fac_a, fac_b,
    wsem, xsem, recv, sent, hop_recv, hop_sent,
):
    sections = lax.axis_size("pipe")
    peers = lax.axis_size("expert")
    s = lax.axis_index("pipe")
    d = lax.axis_index("expert")
    tokens, micros, width = xbuf.shape
    topk = routes.shape[2]
    units = wdn.shape[0]
    tiles = width // LANES
    slots = send_f.shape[2] * CAP
    pairs = peers * CAP
    last = sections - 1
    span = peers // CHUNKS
    y, z = d >> 3, d & (NZ - 1)
    side = 1 - 2 * (s & 1)

    load_in = pltpu.make_async_copy(win_hbm.at[0], win, wsem.at[0])
    load_down = pltpu.make_async_copy(wdn_hbm.at[0], wdn, wsem.at[1])
    load_x = pltpu.make_async_copy(x_hbm, xbuf, xsem)
    load_g = pltpu.make_async_copy(gin_hbm, xbuf, xsem)

    @pl.when(s == 0)
    def _():
        load_x.start()

    @pl.when(s == last)
    def _():
        load_g.start()

    load_in.start()
    load_down.start()

    barrier = pltpu.get_barrier_semaphore()

    def greet(i, carry):
        pl.semaphore_signal(barrier, inc=1, device_id=(s, lax.rem(d + i, peers)), device_id_type=MESH)
        return carry

    lax.fori_loop(1, peers, greet, 0)

    @pl.when(s > 0)
    def _():
        pl.semaphore_signal(barrier, inc=1, device_id=(s - 1, d), device_id_type=MESH)

    @pl.when(s < last)
    def _():
        pl.semaphore_signal(barrier, inc=1, device_id=(s + 1, d), device_id_type=MESH)

    pl.semaphore_wait(barrier, peers - 1 + jnp.minimum(s, 1) + jnp.minimum(last - s, 1))

    def spread_rows(dest, m):
        dest[m] = jnp.zeros((ROWS, width), BF)
        dest[m, 0:tokens, :] = xbuf[:, m, :]

    @pl.when(s == 0)
    def _():
        load_x.wait()
        for m in range(micros):
            spread_rows(hid, m)

    @pl.when(s == last)
    def _():
        load_g.wait()
        for m in range(micros):
            spread_rows(gout, m)

    def place_of(i):
        pair, inner = i >> 3, i & 7
        far = jnp.where(pair == 0, 3, jnp.where(pair == 1, 4, 4 - pair))
        near = jnp.where(pair == 0, 5, jnp.where(pair == 1, 0, 4 + pair))
        dz = jnp.where((inner & 1) == 0, far, near)
        rank = inner >> 1
        dy = jnp.where(rank == 0, 2, jnp.where(rank == 1, 1, jnp.where(rank == 2, 3, 0)))
        return dy * side, dz * side

    def onward(i):
        dy, dz = place_of(i)
        return (((y + dy) & (NY - 1)) << 3) + ((z + dz) & (NZ - 1))

    def homeward(i):
        dy, dz = place_of(i)
        return (((y - dy) & (NY - 1)) << 3) + ((z - dz) & (NZ - 1))

    def chosen(m):
        ids = [routes[0, m, p % topk, p // topk] for p in range(tokens * topk)]
        found = []
        for p, e in enumerate(ids):
            place = jnp.int32(0)
            for q in range(p):
                place = place + jnp.where(ids[q] == e, 1, 0)
            found.append((p // topk, e * CAP + place, gates[0, m, p % topk, p // topk]))
        return found

    def by_slot(m, weighted):
        count = 2 * slots if weighted else slots
        row = lax.broadcasted_iota(jnp.int32, (count, ROWS), 0)
        col = lax.broadcasted_iota(jnp.int32, (count, ROWS), 1)
        table = jnp.zeros((count, ROWS), F32)
        for t, slot, gate in chosen(m):
            hit = ((row & (slots - 1)) == slot) & (col == t)
            table = jnp.where(hit, gate if weighted else 1.0, table)
        if weighted:
            high = table.astype(BF).astype(F32)
            table = jnp.where(row < slots, high, table - high)
        return table.astype(BF)

    def by_token(m, weighted):
        count = 2 * ROWS if weighted else ROWS
        row = lax.broadcasted_iota(jnp.int32, (count, pairs), 0)
        col = lax.broadcasted_iota(jnp.int32, (count, pairs), 1)
        slot_of = ((onward(col >> 1) >> 2) << 1) + (col & 1)
        table = jnp.zeros((count, pairs), F32)
        for t, slot, gate in chosen(m):
            hit = (slot_of == slot) & ((row & (ROWS - 1)) == t)
            table = jnp.where(hit, gate if weighted else 1.0, table)
        if weighted:
            high = table.astype(BF).astype(F32)
            table = jnp.where(row < ROWS, high, table - high)
        return table.astype(BF)

    def dispatch(send, rows, m, phase):
        def start(j, carry):
            i = j + jnp.where(j >= OWN, 1, 0)
            peer = onward(i)
            pltpu.make_async_remote_copy(
                src_ref=send.at[m, :, peer >> 2],
                dst_ref=rows.at[m, :, i],
                send_sem=sent.at[phase, m],
                recv_sem=recv.at[phase, m, i // span],
                device_id=(s, peer),
                device_id_type=MESH,
            ).start()
            return carry

        lax.fori_loop(0, peers - 1, start, 0)
        pltpu.make_async_copy(
            send.at[m, :, d >> 2], rows.at[m, :, OWN], recv.at[phase, m, OWN // span]
        ).start()

    def give_back(out, ret, m, phase, chunk):
        def start(j, carry):
            i = j + jnp.where(j >= OWN, 1, 0)
            pltpu.make_async_remote_copy(
                src_ref=out.at[m, :, i],
                dst_ref=ret.at[m, :, i],
                send_sem=sent.at[phase, m],
                recv_sem=recv.at[phase, m, 0],
                device_id=(s, homeward(i)),
                device_id_type=MESH,
            ).start()
            return carry

        own = OWN // span
        first = chunk * span - jnp.where(chunk > own, 1, 0)
        end = (chunk + 1) * span - jnp.where(chunk >= own, 1, 0)
        lax.fori_loop(first, end, start, 0)

        @pl.when(chunk == own)
        def _():
            pltpu.make_async_copy(
                out.at[m, :, OWN], ret.at[m, :, OWN], recv.at[phase, m, 0]
            ).start()

    def arrived(part, sem):
        pltpu.make_async_copy(part, part, sem).wait()

    def flat(buf, m, count, first, size):
        view = buf.at[m].reshape(tiles, count, LANES)
        return jnp.concatenate([view[k, pl.ds(first, size), :] for k in range(tiles)], axis=1)

    def store_flat(buf, m, count, first, tile, value):
        view = buf.at[m].reshape(tiles, count, LANES)
        size = value.shape[0]
        for k in range(value.shape[1] // LANES):
            view[tile + k, pl.ds(first, size), :] = value[:, k * LANES : (k + 1) * LANES]

    def hop(src, dst, m, way, to):
        return pltpu.make_async_remote_copy(
            src_ref=src.at[m],
            dst_ref=dst.at[m],
            send_sem=hop_sent.at[way, m],
            recv_sem=hop_recv.at[way, m],
            device_id=(to, d),
            device_id_type=MESH,
        )

    def normalize(m):
        values = hid[m].astype(F32)
        inv = lax.rsqrt(jnp.mean(values * values, axis=1, keepdims=True) + norm_eps)
        return values, inv

    def turn_weights():
        for k in range(0, width, WIDE):
            win_t[:, k : k + WIDE] = win[k : k + WIDE, :].T
            wdn_t[k : k + WIDE, :] = wdn[:, k : k + WIDE].T

    def forward_source(m):
        table = by_slot(m, False)

        @pl.when(s > 0)
        def _():
            hop(aout, hid, m, 0, s).wait_recv()

        values, inv = normalize(m)
        normed = (values * inv * gain_ref[...]).astype(BF)
        block = jnp.dot(table, normed, preferred_element_type=F32)
        store_flat(send_f, m, slots, 0, 0, block.astype(BF))
        dispatch(send_f, rows_f, m, 0)

    def forward_chunk(m, chunk):
        size = span * CAP
        first = pl.multiple_of(chunk * size, size)
        arrived(rows_f.at[m, :, pl.ds(chunk * span, span)], recv.at[0, m, chunk])
        pre = jnp.dot(flat(rows_f, m, pairs, first, size), win[...], preferred_element_type=F32)
        gate, up = pre[:, :units], pre[:, units:]
        sigma = jax.nn.sigmoid(gate)
        inner = (gate * sigma * up).astype(BF)
        for k in range(0, width, WIDE):
            part = jnp.dot(inner, wdn[:, k : k + WIDE], preferred_element_type=F32)
            store_flat(out_f, m, pairs, first, k // LANES, part.astype(BF))

        @pl.when(s < last)
        def _():
            give_back(out_f, ret_f, m, 1, chunk)

        fac_a[m, pl.ds(first, size), :] = up * sigma * (1.0 + gate * (1.0 - sigma))
        fac_b[m, pl.ds(first, size), :] = gate * sigma

    def keep(ref, m, result):
        for own in range(micros):

            @pl.when(m == own)
            def _():
                ref[0, :, own, :] = result[:tokens]

    def forward_combine(m):
        table = by_token(m, True)
        arrived(ret_f.at[m], recv.at[1, m, 0])
        both = jnp.dot(table, flat(ret_f, m, pairs, 0, pairs), preferred_element_type=F32)
        result = (hid[m].astype(F32) + (both[:ROWS] + both[ROWS:])).astype(BF)
        aout[m] = result

        @pl.when(s < last)
        def _():
            hop(aout, hid, m, 0, s + 1).start()

        keep(acts_ref, m, result)


    def backward_source(m):
        table = by_slot(m, True)

        @pl.when(s < last)
        def _():
            hop(bout, gout, m, 1, s).wait_recv()

        block = jnp.dot(table, gout[m], preferred_element_type=F32)
        store_flat(send_b, m, slots, 0, 0, (block[:slots] + block[slots:]).astype(BF))
        dispatch(send_b, rows_b, m, 2)

    def backward_chunk(m, chunk):
        size = span * CAP
        first = pl.multiple_of(chunk * size, size)
        arrived(rows_b.at[m, :, pl.ds(chunk * span, span)], recv.at[2, m, chunk])
        d_inner = jnp.dot(
            flat(rows_b, m, pairs, first, size), wdn_t[...], preferred_element_type=F32
        )
        d_both = jnp.concatenate(
            [d_inner * fac_a[m, pl.ds(first, size), :], d_inner * fac_b[m, pl.ds(first, size), :]],
            axis=1,
        ).astype(BF)
        for k in range(0, width, WIDE):
            part = jnp.dot(d_both, win_t[:, k : k + WIDE], preferred_element_type=F32)
            store_flat(out_b, m, pairs, first, k // LANES, part.astype(BF))
        give_back(out_b, ret_b, m, 3, chunk)

    def backward_combine(m):
        values, inv = normalize(m)
        table = by_token(m, False)
        arrived(ret_b.at[m], recv.at[3, m, 0])
        d_normed = jnp.dot(table, flat(ret_b, m, pairs, 0, pairs), preferred_element_type=F32)
        d_scaled = d_normed * gain_ref[...]
        product = jnp.sum(d_scaled * values, axis=1, keepdims=True)
        result = gout[m].astype(F32) + inv * d_scaled - (inv * inv * inv * product / width) * values
        result = result.astype(BF)
        bout[m] = result

        @pl.when(s > 0)
        def _():
            hop(bout, gout, m, 1, s - 1).start()

        keep(grads_ref, m, result)


    def each_chunk(step):
        def body(chunk, carry):
            step(chunk)
            return carry

        lax.fori_loop(0, CHUNKS, body, 0)

    def each(step):
        def body(m, carry):
            step(m)
            return carry

        lax.fori_loop(0, micros, body, 0)

    def weights_ready():
        load_in.wait()
        load_down.wait()

    @pl.when(s > 0)
    def _():
        weights_ready()
        turn_weights()

    @pl.when(s == last)
    def _():
        each(backward_source)

    lag = jnp.minimum(2 * (last - s), micros)
    early = s < EARLY

    @pl.when(s == 0)
    def _():
        forward_source(0)
        weights_ready()

    def tick(k, carry):
        ahead, behind = k < micros, k >= lag

        @pl.when(ahead & ((s > 0) & jnp.logical_not(early & (k > 0)) | (s == 0) & (k > 0) & jnp.logical_not(early)))
        def _():
            forward_source(k)

        @pl.when(behind & (s < last))
        def _():
            backward_source(k - lag)

        @pl.when(ahead)
        def _():
            def both_ways(chunk):
                forward_chunk(k, chunk)

                @pl.when(s == last)
                def _():
                    backward_chunk(k, chunk)

            each_chunk(both_ways)

        @pl.when(early & (k + 1 < micros))
        def _():
            forward_source(k + 1)

        @pl.when(behind & (s < last))
        def _():
            each_chunk(lambda chunk: backward_chunk(k - lag, chunk))

        @pl.when(ahead & (s < last))
        def _():
            forward_combine(k)

        @pl.when((s == 0) & (k == micros - 1))
        def _():
            turn_weights()

        @pl.when(behind)
        def _():
            backward_combine(k - lag)

        return carry

    lax.fori_loop(0, micros + lag, tick, 0)

    @pl.when(s == last)
    def _():
        def reply(m):
            each_chunk(lambda chunk: give_back(out_f, ret_f, m, 1, chunk))

        each(reply)
        each(forward_combine)

    def settle(m, carry):
        for phase in range(4):
            most = out_f.at[m, :, 0 : peers - 1]
            pltpu.make_async_copy(most, most, sent.at[phase, m]).wait()

        @pl.when(s < last)
        def _():
            hop(aout, hid, m, 0, s + 1).wait_send()

        @pl.when(s > 0)
        def _():
            hop(bout, gout, m, 1, s - 1).wait_send()

        return carry

    lax.fori_loop(0, micros, settle, 0)


def local(x_in, grad_in, norm_gain, w_in, w_down, routes, gates):
    peers = lax.axis_size("expert")
    micros, tokens, width = x_in.shape
    cols = w_in.shape[2]
    units = w_down.shape[1]
    tiles = width // LANES
    out = jax.ShapeDtypeStruct((1, tokens, micros, width), BF)
    small = pltpu.VMEM((micros, tiles, peers // GROUP, CAP, LANES), BF)
    large = pltpu.VMEM((micros, tiles, peers, CAP, LANES), BF)
    state = pltpu.VMEM((micros, ROWS, width), BF)
    factor = pltpu.VMEM((micros, peers * CAP, units), F32)
    anywhere = pl.BlockSpec(memory_space=pl.ANY)
    vmem = pl.BlockSpec(memory_space=pltpu.VMEM)
    smem = pl.BlockSpec(memory_space=pltpu.SMEM)
    acts, grads = pl.pallas_call(
        layer_kernel,
        out_shape=(out, out),
        in_specs=[anywhere, anywhere, vmem, anywhere, anywhere, smem, smem],
        out_specs=(vmem, vmem),
        scratch_shapes=[
            pltpu.VMEM((width, cols), BF),
            pltpu.VMEM((units, width), BF),
            pltpu.VMEM((cols, width), BF),
            pltpu.VMEM((width, units), BF),
            pltpu.VMEM((tokens, micros, width), BF),
            state, state, state, state,
            small, large, large, large,
            small, large, large, large,
            factor, factor,
            pltpu.SemaphoreType.DMA((2,)),
            pltpu.SemaphoreType.DMA,
            pltpu.SemaphoreType.DMA((4, micros, CHUNKS)),
            pltpu.SemaphoreType.DMA((4, micros)),
            pltpu.SemaphoreType.DMA((2, micros)),
            pltpu.SemaphoreType.DMA((2, micros)),
        ],
        compiler_params=pltpu.CompilerParams(
            collective_id=0, has_side_effects=True, vmem_limit_bytes=56 << 20
        ),
    )(
        jnp.swapaxes(x_in, 0, 1),
        jnp.swapaxes(grad_in, 0, 1),
        norm_gain,
        w_in,
        w_down,
        jnp.swapaxes(routes, 2, 3),
        jnp.swapaxes(gates, 2, 3),
    )
    return jnp.swapaxes(acts, 1, 2), jnp.swapaxes(grads, 1, 2)


def solution(mesh):
    placed = (
        P(None, "expert", None),
        P(None, "expert", None),
        P("pipe", None),
        P("pipe", None, "expert"),
        P("pipe", "expert", None),
        P("pipe", None, "expert", None),
        P("pipe", None, "expert", None),
    )
    return jax.shard_map(
        local,
        mesh=mesh,
        in_specs=placed,
        out_specs=(P("pipe", None, "expert", None), P("pipe", None, "expert", None)),
        check_vma=False,
    )
```
